128 devices in a mesh: expert: 16 (over y, z), replica: 4 (over x), tensor: 2 (over core).
Axes of the slice: x: 4, y: 4, z: 4, core: 2. Of those that a mesh axis runs over, the one named last changes fastest.
Arguments:
- tokens: bfloat16 [8192, 2048], P(('expert', 'replica')), may hold values from -6 to 6
- cotangent: bfloat16 [8192, 2048], P(('expert', 'replica')), may hold values from -6 to 6
- routes: int32 [8192, 8], P(('expert', 'replica')), may hold values from 0 to 63, all different within a row; in each aligned block of 128 rows (0 to 127, 128 to 255, ...) at most 32 rows name the same one
- gates: float32 [8192, 8], P(('expert', 'replica')), may hold values from 0.05 to 1
- gate_weight: bfloat16 [64, 2048, 768], P('expert', None, 'tensor'), may hold values from -0.125 to 0.125
- up_weight: bfloat16 [64, 2048, 768], P('expert', None, 'tensor'), may hold values from -0.125 to 0.125
- down_weight: bfloat16 [64, 768, 2048], P('expert', 'tensor'), may hold values from -0.21875 to 0.21875
Outputs:
- token_grad: bfloat16 [8192, 2048], P(('expert', 'replica'), 'tensor')
- gate_weight_grad: bfloat16 [64, 2048, 768], P(('expert', 'replica'), None, 'tensor')
- up_weight_grad: bfloat16 [64, 2048, 768], P(('expert', 'replica'), None, 'tensor')
- down_weight_grad: bfloat16 [64, 768, 2048], P(('expert', 'replica'), 'tensor')
The draws below stay inside these ranges and needn't reach their ends.
Inputs may be any that keep to these rules, and one draw needn't show every extreme that they name: `routes`: each row names 8 different experts. Within each aligned block of 128 rows (the rows of one device) no expert is named by more than 32 rows, a bound that some block reaches.
All inputs are finite; a program needn't handle non-finite values.
Results may differ from the reference program's by a relative error of at most 0.0095.
Values may be sent and summed in bfloat16 or wider, within the bound.
A program may use at most 192 MiB of HBM per device.

```python
import math
import jax
import jax.numpy as jnp
import numpy as np
from jax import lax

D = 2048
FF = 768
TOPK = 8
TOK_DEV = 128
EXPERTS = 64
TOKENS = 8192
CAP = 32
N_EXPERT = 16
N_REPLICA = 4
N_TENSOR = 2


def level_of(rng, extent, shards, low, top_value):
    level, own = 1.0, jax.random.fold_in(rng, 6)
    for dim, blocks in shards:
        steps = jnp.exp(jax.random.uniform(jax.random.fold_in(own, dim), (blocks,), jnp.float32, low / len(shards), top_value / len(shards)))
        level = level * jnp.repeat(steps, extent[dim] // blocks).reshape([-1 if axis == dim else 1 for axis in range(len(extent))])
    return level


def deal_out(rng, own, number, rows, count, top, reach, lean):
    order = jax.random.permutation(rng, count)
    crowded, ordinary = shares(count, rows * top, reach, lean, True), shares(count, rows * top, reach, lean, False)
    places = jnp.arange(count)

    def named(sizes, rotation):
        used = int((sizes > 0).sum())
        fixed = max(1, used // 4)
        passed = fixed + (places - fixed + rotation * (used - fixed)) % max(1, count - fixed)
        return jnp.zeros((count,), jnp.int32).at[order[jnp.where(places < fixed, places, passed)]].set(jnp.asarray(sizes, jnp.int32))

    sizes = jnp.where(number % 4 == 0, named(crowded, number // 4), named(ordinary, number - number // 4 - 1))
    mixed = jax.random.permutation(jax.random.fold_in(own, 3), count)
    donor, receiver = mixed[0:count // 2 * 2:2], mixed[1:count // 2 * 2:2]
    margin = jnp.minimum(sizes[donor] - 1, reach - sizes[receiver]) // 2
    margin = jnp.where((donor == order[0]) | (receiver == order[0]) | (sizes[receiver] == 0), 0, jnp.maximum(margin, 0))
    passed = jax.random.randint(jax.random.fold_in(own, 4), (count // 2,), 0, 1 << 20) % (margin + 1)
    sizes = sizes.at[donor].add(-passed).at[receiver].add(passed)
    members = jnp.searchsorted(jnp.cumsum(sizes), jnp.arange(rows * top), side="right").astype(jnp.int32)
    table = members.reshape(top, rows).T
    table = table[jax.random.permutation(jax.random.fold_in(own, 1), rows)]
    rotation = jax.random.randint(jax.random.fold_in(own, 2), (rows, 1), 0, top)
    return jnp.take_along_axis(table, (jnp.arange(top)[None, :] + rotation) % top, axis=1)


def shares(amount, total, limit, lean, full):
    portions = [(1 << 20) // math.isqrt(standing ** lean) + 1 for standing in range(1, amount + 1)]
    largest = limit if full else min(limit, max(-(-total // amount), total * portions[0] // sum(portions)))
    least = 1 if total - largest >= amount - 1 else 0
    holding, surplus = [largest] + [least] * (amount - 1), total - largest - least * (amount - 1)
    while surplus > 0:
        movable = [i for i in range(1, amount) if holding[i] < largest] or [i for i in range(1, amount) if holding[i] < limit]
        whole, left = sum([portions[i] for i in movable]), surplus
        for i in movable:
            extra = min(limit - holding[i], max(1, left * portions[i] // whole), surplus)
            holding[i] = holding[i] + extra
            surplus = surplus - extra
    return np.array(holding)


def centred(rng, extent, scale, most, split=(), held_as=jnp.bfloat16):
    gain = level_of(rng, extent, split, -0.22, 0.18) if split else 1.0
    result = jax.random.normal(rng, extent, jnp.float32) * scale * gain
    return jnp.minimum(jnp.maximum(result, -most), most).astype(held_as)


def setup_inputs(seed: int = 0) -> dict:
    seeds = jax.random.split(jax.random.key(seed), 8)
    tokens = centred(seeds[0], (TOKENS, D), 1.0, 6.0, ((0, 64),))
    cotangent = centred(seeds[1], (TOKENS, D), 1.0, 6.0, ((0, 64),))
    routes_keys = jax.random.split(jax.random.fold_in(seeds[2], 1), TOKENS // TOK_DEV)
    routes_turns = jax.random.permutation(jax.random.fold_in(seeds[2], 3), TOKENS // TOK_DEV)
    routes = jax.vmap(lambda own, number: deal_out(jax.random.fold_in(seeds[2], 2), own, number, TOK_DEV, EXPERTS, TOPK, CAP, 2))(routes_keys, routes_turns).reshape((TOKENS, TOPK))
    gates = jnp.clip(jnp.exp(math.log(1.0) - 2.9957323 * jax.random.uniform(seeds[3], (TOKENS, TOPK), jnp.float32) ** level_of(seeds[3], (TOKENS, TOPK), ((0, 64),), -0.2, 0.2)), 0.05, 1.0)
    gate_weight = centred(seeds[4], (EXPERTS, D, FF), D ** -0.5, 0.125, ((0, 16), (2, 2)))
    up_weight = centred(seeds[5], (EXPERTS, D, FF), D ** -0.5, 0.125, ((0, 16), (2, 2)))
    down_weight = centred(seeds[6], (EXPERTS, FF, D), FF ** -0.5, 0.21875, ((0, 16), (1, 2)))
    return {"tokens": tokens, "cotangent": cotangent, "routes": routes, "gates": gates, "gate_weight": gate_weight, "up_weight": up_weight, "down_weight": down_weight}


def slot_ranks(block_routes):
    one_hot = (block_routes[:, None] == jnp.arange(EXPERTS, dtype=jnp.int32)[None, :]).astype(jnp.int32)
    earlier = jnp.cumsum(one_hot, axis=0) - one_hot
    return jnp.sum(earlier * one_hot, axis=1).astype(jnp.int32)


def replica_sum(left, right):
    left_groups = left.reshape(N_EXPERT, N_REPLICA, CAP, left.shape[1]).astype(jnp.float32)
    right_groups = right.reshape(N_EXPERT, N_REPLICA, CAP, right.shape[1]).astype(jnp.float32)
    partial_value = jnp.einsum("srca,srcb->rab", left_groups, right_groups).astype(jnp.bfloat16)
    partial_value = lax.optimization_barrier(partial_value)
    return jnp.sum(partial_value.astype(jnp.float32), axis=0).astype(jnp.bfloat16)


def reference(tokens, cotangent, routes, gates, gate_weight, up_weight, down_weight):
    blocks = N_EXPERT * N_REPLICA
    slots_all = blocks * CAP
    per_block = routes.reshape(blocks, TOK_DEV * TOPK)
    slot_rank = jax.vmap(slot_ranks)(per_block)
    block_ids = jnp.arange(blocks, dtype=jnp.int32)[:, None]
    position = (block_ids * CAP + slot_rank).reshape(-1).astype(jnp.int32)
    chosen = routes.reshape(-1).astype(jnp.int32)
    pair_ids = jnp.arange(chosen.shape[0], dtype=jnp.int32)
    row_table = jnp.zeros((EXPERTS, slots_all), jnp.int32).at[chosen, position].set(pair_ids)
    live_table = jnp.zeros((EXPERTS, slots_all), jnp.int32).at[chosen, position].set(1)
    flat_gates = gates.reshape(-1)
    half = FF // N_TENSOR

    def one_expert(grad_total, packed):
        row_ids, live_rows, w_gate, w_up, w_down = packed
        token_ids = (row_ids // TOPK).astype(jnp.int32)
        keep = live_rows[:, None] > 0
        in_rows = jnp.where(keep, tokens[token_ids], jnp.zeros((), tokens.dtype))
        gain_rows = jnp.where(live_rows > 0, flat_gates[row_ids], jnp.zeros((), flat_gates.dtype))
        cot_rows = (gain_rows[:, None].astype(jnp.float32) * cotangent[token_ids].astype(jnp.float32)).astype(jnp.bfloat16)
        gate_parts = []
        up_parts = []
        down_parts = []
        slot_total = jnp.zeros((slots_all, D), jnp.float32)
        for half_index in range(N_TENSOR):
            col_start = half_index * half
            gate_cols = w_gate[:, col_start:col_start + half]
            up_cols = w_up[:, col_start:col_start + half]
            down_rows = w_down[col_start:col_start + half, :]
            gate_pre = jnp.dot(in_rows, gate_cols, preferred_element_type=jnp.float32)
            up_proj = jnp.dot(in_rows, up_cols, preferred_element_type=jnp.float32)
            hidden_grad = jnp.dot(cot_rows, down_rows.T, preferred_element_type=jnp.float32)
            sig_gate = jax.nn.sigmoid(gate_pre)
            activated = gate_pre * sig_gate
            hidden = (activated * up_proj).astype(jnp.bfloat16)
            gate_grad = (hidden_grad * up_proj * sig_gate * (1.0 + gate_pre * (1.0 - sig_gate))).astype(jnp.bfloat16)
            up_grad = (hidden_grad * activated).astype(jnp.bfloat16)
            row_grads = (jnp.dot(gate_grad, gate_cols.T, preferred_element_type=jnp.float32)
                         + jnp.dot(up_grad, up_cols.T, preferred_element_type=jnp.float32)).astype(jnp.bfloat16)
            slot_total = slot_total + row_grads.astype(jnp.float32)
            gate_parts.append(replica_sum(in_rows, gate_grad))
            up_parts.append(replica_sum(in_rows, up_grad))
            down_parts.append(replica_sum(hidden, cot_rows))
        slot_grads = slot_total.astype(jnp.bfloat16)
        grad_total = grad_total.at[token_ids].add(slot_grads.astype(jnp.float32))
        return grad_total, (jnp.concatenate(gate_parts, axis=1), jnp.concatenate(up_parts, axis=1),
                            jnp.concatenate(down_parts, axis=0))

    start_total = jnp.zeros((TOKENS, D), jnp.float32)
    grad_total, stacked = lax.scan(one_expert, start_total,
                                   (row_table, live_table, gate_weight, up_weight, down_weight))
    return grad_total.astype(jnp.bfloat16), stacked[0], stacked[1], stacked[2]
```

```python
import functools

import jax
import jax.numpy as jnp
from jax import lax
from jax.experimental import pallas as pl
from jax.experimental.pallas import tpu as pltpu
from jax.sharding import PartitionSpec as P

MESH = pl.DeviceIdType.MESH
CAP = 32
BF = jnp.bfloat16


def gray(i):
    return i + i // 2 - 2 * (i // 3)


def dispatch_kernel(src_ref, meta_ref, out_ref, ag, mag, stage, rows,
                    ag_s, ag_r, mg_s, mg_r, x_s, x_r, f_s, f_r, o_s):
    e = lax.axis_index("expert")
    x = lax.axis_index("replica")
    c = lax.axis_index("tensor")
    y, z = e // 4, e % 4
    first = c == 0
    width = src_ref.shape[1]

    def chip(dy, dz):
        return ((y + dy) % 4) * 4 + (z + dz) % 4

    def axis_a(d):
        return jnp.where(first, 0, d), jnp.where(first, d, 0)

    def axis_b(d):
        return jnp.where(first, d, 0), jnp.where(first, 0, d)

    barrier = pltpu.get_barrier_semaphore()
    for d in (1, 2, 3):
        for dev in ((chip(0, d), x, c), (chip(d, 0), x, c), (e, (x + d) % 4, c)):
            pl.semaphore_signal(barrier, inc=1, device_id=dev, device_id_type=MESH)
    pl.semaphore_signal(barrier, inc=1, device_id=(e, x, 1 - c), device_id_type=MESH)
    pl.semaphore_wait(barrier, 10)

    def block_copies(src, msrc, by, bz, ty, tz, slot):
        home = chip(by, bz)
        landed = ((by - ty + 4) % 4) * 4 + (bz - tz + 4) % 4
        dev = (chip(ty, tz), x, c)
        return (
            pltpu.make_async_remote_copy(src_ref=msrc, dst_ref=mag.at[home], send_sem=mg_s.at[slot],
                                         recv_sem=mg_r.at[landed], device_id=dev, device_id_type=MESH),
            pltpu.make_async_remote_copy(src_ref=src, dst_ref=ag.at[home], send_sem=ag_s.at[slot],
                                         recv_sem=ag_r.at[landed], device_id=dev, device_id_type=MESH),
        )

    def wait_block(by, bz):
        rel = by * 4 + bz
        for cp in (
            pltpu.make_async_remote_copy(src_ref=meta_ref, dst_ref=mag.at[chip(by, bz)], send_sem=mg_s.at[0],
                                         recv_sem=mg_r.at[rel], device_id=(e, x, 1 - c), device_id_type=MESH),
            pltpu.make_async_remote_copy(src_ref=src_ref, dst_ref=ag.at[chip(by, bz)], send_sem=ag_s.at[0],
                                         recv_sem=ag_r.at[rel], device_id=(e, x, 1 - c), device_id_type=MESH),
        ):
            cp.wait_recv()

    for i, d in enumerate((1, 3, 2)):
        for ax, base in ((axis_a, 0), (axis_b, 3)):
            ty, tz = ax(d)
            for cp in block_copies(src_ref, meta_ref, 0, 0, ty, tz, base + i):
                cp.start()
    ag[e] = src_ref[...]
    mag[e] = meta_ref[...]

    def x_copy(r, home, d):
        return pltpu.make_async_remote_copy(
            src_ref=stage.at[r, (x + d) % 4], dst_ref=rows.at[c, home, x], send_sem=x_s.at[r * 3 + d - 1],
            recv_sem=x_r.at[r * 3 + d - 1], device_id=(e, (x + d) % 4, c), device_id_type=MESH)

    def x_landed(r, home, d):
        return pltpu.make_async_remote_copy(
            src_ref=stage.at[r, 0], dst_ref=rows.at[c, home, (x - d + 4) % 4], send_sem=x_s.at[r * 3 + d - 1],
            recv_sem=x_r.at[r * 3 + d - 1], device_id=(e, (x + d) % 4, c), device_id_type=MESH)

    def forward(r, home, kind):
        return pltpu.make_async_remote_copy(
            src_ref=rows.at[kind, home], dst_ref=rows.at[kind, home], send_sem=f_s.at[r], recv_sem=f_r.at[r],
            device_id=(e, x, 1 - c), device_id_type=MESH)

    def put(r, home, kind):
        return pltpu.make_async_copy(rows.at[kind, home], out_ref.at[kind, home], o_s.at[kind, r])

    slot_ids = lax.broadcasted_iota(jnp.int32, (CAP, 128), 0).astype(jnp.float32)

    def pick(r, home):
        m = mag[home, e].astype(jnp.float32)
        gsum = m[4:8] + m[8:12] + m[12:16]
        sel, scale = [], []
        for j in range(4):
            s = jnp.where(slot_ids == m[j:j + 1], 1.0, 0.0)
            sel.append(s)
            scale.append(jnp.sum(s * gsum[j:j + 1], axis=1, keepdims=True))
        sel = jnp.concatenate(sel, axis=0).astype(BF)
        scale = jnp.concatenate(scale, axis=0)
        scale = jnp.where(first, jnp.ones_like(scale), scale)
        for t in range(0, width, 512):
            got = jnp.dot(sel, ag[home, :, t:t + 512], preferred_element_type=jnp.float32) * scale
            stage[r, :, :, t:t + 512] = got.astype(BF).reshape(4, CAP, 512)

    lag = 2

    def finish(r):
        home = chip(gray(r // 4), gray(r % 4))
        for d in (1, 2, 3):
            x_landed(r, home, d).wait_recv()
        forward(r, home, c).start()
        put(r, home, c).start()

    def step(r, carry):
        dy, dz = gray(r // 4), gray(r % 4)
        home = chip(dy, dz)

        @pl.when((r >= 1) & (r <= 3))
        def _():
            ay, az = axis_a(gray(r % 4))
            wait_block(ay, az)
            for i, d in enumerate((1, 3, 2)):
                ty, tz = axis_b(d)
                for cp in block_copies(ag.at[chip(ay, az)], mag.at[chip(ay, az)], ay, az, ty, tz, 3 + r * 3 + i):
                    cp.start()

        @pl.when(jnp.where(first, dy, dz) != 0)
        def _():
            wait_block(dy, dz)

        pick(r, home)
        for d in (1, 3, 2):
            x_copy(r, home, d).start()
        rows[c, home, x] = stage[r, x]

        @pl.when(r >= lag)
        def _():
            finish(r - lag)
        return carry

    lax.fori_loop(0, 16, step, 0)
    for r in range(16 - lag, 16):
        finish(r)

    def drain(r, carry):
        home = chip(gray(r // 4), gray(r % 4))
        forward(r, home, 1 - c).wait_recv()
        put(r, home, 1 - c).start()
        return carry

    lax.fori_loop(0, 16, drain, 0)

    def close(r, carry):
        home = chip(gray(r // 4), gray(r % 4))
        forward(r, home, c).wait_send()
        put(r, home, 0).wait()
        put(r, home, 1).wait()
        for d in (1, 2, 3):
            x_copy(r, home, d).wait_send()
        return carry

    lax.fori_loop(0, 16, close, 0)
    for slot in range(15):
        for cp in block_copies(src_ref, meta_ref, 0, 0, 0, 1, slot):
            cp.wait_send()


def dispatch(src, meta):
    width = src.shape[1]
    return pl.pallas_call(
        dispatch_kernel,
        out_shape=jax.ShapeDtypeStruct((2, 16, 4, CAP, width), BF),
        in_specs=[pl.BlockSpec(memory_space=pltpu.VMEM)] * 2,
        out_specs=pl.BlockSpec(memory_space=pl.ANY),
        scratch_shapes=[
            pltpu.VMEM((16, 128, width), BF),
            pltpu.VMEM((16, 16, 16, 128), BF),
            pltpu.VMEM((16, 4, CAP, width), BF),
            pltpu.VMEM((2, 16, 4, CAP, width), BF),
            pltpu.SemaphoreType.DMA((15,)),
            pltpu.SemaphoreType.DMA((16,)),
            pltpu.SemaphoreType.DMA((15,)),
            pltpu.SemaphoreType.DMA((16,)),
            pltpu.SemaphoreType.DMA((48,)),
            pltpu.SemaphoreType.DMA((48,)),
            pltpu.SemaphoreType.DMA((16,)),
            pltpu.SemaphoreType.DMA((16,)),
            pltpu.SemaphoreType.DMA((2, 16)),
        ],
        compiler_params=pltpu.CompilerParams(collective_id=0, has_side_effects=True, vmem_limit_bytes=48 * 2**20),
    )(src, meta)


def routing(routes, gates):
    ids = jnp.arange(64, dtype=jnp.int32)
    hit = ids[:, None, None] == routes.T[None]
    mask = jnp.sum(hit.astype(jnp.float32), axis=1)
    gmap = jnp.sum(jnp.where(hit, gates.T[None], 0.0), axis=1)
    before = jnp.triu(jnp.ones((128, 128), BF), 1)
    rank = jnp.dot(mask.astype(BF), before, preferred_element_type=jnp.float32)
    rank = jnp.where(mask > 0, rank, 64.0)
    high = lax.reduce_precision(gmap, 8, 7)
    rest = gmap - high
    mid = lax.reduce_precision(rest, 8, 7)
    low = rest - mid
    return rank, jnp.stack([rank, high, mid, low]).astype(BF)


def body(tokens, cotangent, routes, gates, gate_weight, up_weight, down_weight):
    width = tokens.shape[1]
    x = lax.axis_index("replica")
    c = lax.axis_index("tensor")
    rank, maps = routing(routes, gates)
    meta = maps.reshape(4, 16, 4, 128).transpose(1, 0, 2, 3).reshape(16, 16, 128)
    rows = dispatch(jnp.where(c == 0, tokens, cotangent), meta)
    rows_in = rows[0].reshape(2048, width)
    cots_in = rows[1].reshape(2048, width)
    w_gate, w_up, w_down = gate_weight[x], up_weight[x], down_weight[x]
    f32 = dict(preferred_element_type=jnp.float32)
    gate_pre = jnp.dot(rows_in, w_gate, **f32)
    up_proj = jnp.dot(rows_in, w_up, **f32)
    hidden_grad = jnp.dot(cots_in, w_down.T, **f32)
    sig = jax.nn.sigmoid(gate_pre)
    act = gate_pre * sig
    hidden = (act * up_proj).astype(BF)
    gate_grad = (hidden_grad * up_proj * sig * (1.0 + gate_pre * (1.0 - sig))).astype(BF)
    up_grad = (hidden_grad * act).astype(BF)
    row_grads = (jnp.dot(gate_grad, w_gate.T, **f32) + jnp.dot(up_grad, w_up.T, **f32)).astype(BF)
    g_gate = jnp.dot(rows_in.T, gate_grad, **f32).astype(BF)
    g_up = jnp.dot(rows_in.T, up_grad, **f32).astype(BF)
    g_down = jnp.dot(hidden.T, cots_in, **f32).astype(BF)

    halves = lax.psum_scatter(row_grads, "tensor", scatter_dimension=1, tiled=True)
    back = lax.all_to_all(halves.reshape(16, 128, width // 2), "expert", split_axis=0, concat_axis=0, tiled=True)
    back = back.reshape(16, 4, CAP, width // 2)
    all_rank = lax.all_gather(rank.astype(BF), "replica", axis=0)
    own = lax.dynamic_index_in_dim(all_rank.reshape(4, 16, 4, 128), x, 2, keepdims=False)
    place = (own[:, :, None, :] == jnp.arange(CAP, dtype=jnp.float32)[None, None, :, None]).astype(BF)
    sums = jnp.einsum("bgst,gbsd->btd", place, back, preferred_element_type=jnp.float32).astype(BF)
    token_grad = lax.psum_scatter(sums, "replica", scatter_dimension=0, tiled=True)
    return token_grad.reshape(128, width // 2), g_gate[None], g_up[None], g_down[None]


def solution(mesh):
    in_specs = (
        P(("expert", "replica"), None),
        P(("expert", "replica"), None),
        P(("expert", "replica"), None),
        P(("expert", "replica"), None),
        P("expert", None, "tensor"),
        P("expert", None, "tensor"),
        P("expert", "tensor", None),
    )
    out_specs = (
        P(("expert", "replica"), "tensor"),
        P(("expert", "replica"), None, "tensor"),
        P(("expert", "replica"), None, "tensor"),
        P(("expert", "replica"), "tensor", None),
    )
    return jax.shard_map(body, mesh=mesh, in_specs=in_specs, out_specs=out_specs, check_vma=False)
```

```python
import jax
import jax.numpy as jnp
from jax import lax
from jax.experimental import pallas as pl
from jax.experimental.pallas import tpu as pltpu
from jax.sharding import PartitionSpec as P

MESH = pl.DeviceIdType.MESH
CAP = 32
BF = jnp.bfloat16
F32 = jnp.float32
LAG = 3
SLOTS = 8


def gray(i):
    return i + i // 2 - 2 * (i // 3)


def dot(a, b, ca, cb):
    return lax.dot_general(a, b, (((ca,), (cb,)), ((), ())), preferred_element_type=F32)


def layer_kernel(src_ref, meta_ref, rank_ref, wg_ref, wu_ref, wd_ref,
                 tok_ref, og_ref, ou_ref, od_ref,
                 ag, mag, stage, rows, wgu, wd, hid, grads, gu, hg, psend, precv, own, back,
                 xrank, place, xsend, xrecv, gtile, dtile,
                 ag_s, ag_r, mg_s, mg_r, x_s, x_r, f_s, f_r, p_s, p_r, b_s, b_r, k_s, k_r, t_s, t_r, w_s, og_s, od_s):
    e = lax.axis_index("expert")
    x = lax.axis_index("replica")
    c = lax.axis_index("tensor")
    y, z = e // 4, e % 4
    first = c == 0
    width = src_ref.shape[1]
    half = width // 2
    hidden = wd.shape[0]

    def chip(dy, dz):
        return ((y + dy) % 4) * 4 + (z + dz) % 4

    def remote(src, dst, send, recv, dev):
        return pltpu.make_async_remote_copy(src_ref=src, dst_ref=dst, send_sem=send, recv_sem=recv,
                                            device_id=dev, device_id_type=MESH)

    def axis_a(d):
        return jnp.where(first, 0, d), jnp.where(first, d, 0)

    def axis_b(d):
        return jnp.where(first, d, 0), jnp.where(first, 0, d)

    partner = (e, x, 1 - c)

    def weights():
        return (pltpu.make_async_copy(wg_ref.at[x], wgu.at[:, pl.ds(0, hidden)], w_s.at[0]),
                pltpu.make_async_copy(wu_ref.at[x], wgu.at[:, pl.ds(hidden, hidden)], w_s.at[1]),
                pltpu.make_async_copy(wd_ref.at[x], wd, w_s.at[2]))

    for cp in weights():
        cp.start()

    barrier = pltpu.get_barrier_semaphore()
    for rel in range(1, 16):
        pl.semaphore_signal(barrier, inc=1, device_id=(chip(rel // 4, rel % 4), x, c), device_id_type=MESH)
    for d in (1, 2, 3):
        pl.semaphore_signal(barrier, inc=1, device_id=(e, (x + d) % 4, c), device_id_type=MESH)
    pl.semaphore_signal(barrier, inc=1, device_id=partner, device_id_type=MESH)
    pl.semaphore_wait(barrier, 19)

    def block_copies(src, msrc, by, bz, ty, tz, slot):
        home = chip(by, bz)
        landed = ((by - ty + 4) % 4) * 4 + (bz - tz + 4) % 4
        dev = (chip(ty, tz), x, c)
        return (remote(msrc, mag.at[home], mg_s.at[slot], mg_r.at[landed], dev),
                remote(src, ag.at[home], ag_s.at[slot], ag_r.at[landed], dev))

    def wait_block(by, bz):
        rel, home = by * 4 + bz, chip(by, bz)
        remote(meta_ref, mag.at[home], mg_s.at[0], mg_r.at[rel], partner).wait_recv()
        remote(src_ref, ag.at[home], ag_s.at[0], ag_r.at[rel], partner).wait_recv()

    for i, d in enumerate((1, 3, 2)):
        for ax, base in ((axis_a, 0), (axis_b, 3)):
            ty, tz = ax(d)
            for cp in block_copies(src_ref, meta_ref, 0, 0, ty, tz, base + i):
                cp.start()

    def rank_copy(d):
        return remote(rank_ref.at[(x + d) % 4], xrank.at[x], k_s.at[d - 1], k_r.at[d - 1], (e, (x + d) % 4, c))

    def rank_landed(d):
        return remote(rank_ref.at[0], xrank.at[(x - d + 4) % 4], k_s.at[d - 1], k_r.at[d - 1], partner)

    for d in (1, 2, 3):
        rank_copy(d).start()
    xrank[x] = rank_ref[x]
    ag[e] = src_ref[...]
    mag[e] = meta_ref[...]

    def x_copy(r, home, d):
        return remote(stage.at[r % SLOTS, (x + d) % 4], rows.at[c, home, x], x_s.at[r * 3 + d - 1],
                      x_r.at[r * 3 + d - 1], (e, (x + d) % 4, c))

    def x_landed(r, home, d):
        return remote(stage.at[0, 0], rows.at[c, home, (x - d + 4) % 4], x_s.at[r * 3 + d - 1],
                      x_r.at[r * 3 + d - 1], partner)

    def forward(r, home, kind):
        return remote(rows.at[kind, home], rows.at[kind, home], f_s.at[r], f_r.at[r], partner)

    slot_ids = lax.broadcasted_iota(jnp.int32, (CAP, 128), 0).astype(F32)

    def pick(r, home):
        m = mag[home, e].astype(F32)
        gsum = m[4:8] + m[8:12] + m[12:16]
        sel, scale = [], []
        for j in range(4):
            s = jnp.where(slot_ids == m[j:j + 1], 1.0, 0.0)
            sel.append(s)
            scale.append(jnp.sum(s * gsum[j:j + 1], axis=1, keepdims=True))
        sel = jnp.concatenate(sel, axis=0).astype(BF)
        scale = jnp.concatenate(scale, axis=0)
        scale = jnp.where(first, jnp.ones_like(scale), scale)
        for t in range(0, width, 512):
            got = dot(sel, ag[home, :, t:t + 512], 1, 0) * scale
            stage[r % SLOTS, :, :, t:t + 512] = got.astype(BF).reshape(4, CAP, 512)

    def pair_copy(q):
        return remote(psend.at[q % 2], precv.at[q], p_s.at[q], p_r.at[q], partner)

    def back_copy(q, dz):
        landed = ((4 - q) % 4) * 4 + (4 - dz) % 4
        return remote(precv.at[q, (z + dz) % 4], back.at[e], b_s.at[q * 4 + dz], b_r.at[landed],
                      (chip(q, dz), x, c))

    def back_landed(dy, dz):
        return remote(precv.at[0, 0], back.at[chip(dy, dz)], b_s.at[0], b_r.at[dy * 4 + dz], partner)

    def chunk(q):
        ya = (y + q) % 4
        for i in range(4):
            r = q * 4 + i
            forward(r, chip(q, gray(i)), 1 - c).wait_recv()

        @pl.when(q == 0)
        def _():
            for cp in weights():
                cp.wait()

        gu[...] = dot(rows[0, pl.ds(ya * 4, 4)].reshape(512, width), wgu[...], 1, 0)
        hg[...] = dot(rows[1, pl.ds(ya * 4, 4)].reshape(512, width), wd[...], 1, 1)

        def act(i, carry):
            at = pl.multiple_of(i * 128, 128)
            to = pl.multiple_of(ya * 512 + i * 128, 128)
            for t in range(0, hidden, 128):
                g = gu[pl.ds(at, 128), t:t + 128]
                u = gu[pl.ds(at, 128), hidden + t:hidden + t + 128]
                h = hg[pl.ds(at, 128), t:t + 128]
                s = jax.nn.sigmoid(g)
                a = g * s
                hid[pl.ds(to, 128), t:t + 128] = (a * u).astype(BF)
                grads[pl.ds(to, 128), t:t + 128] = (h * u * s * (1.0 + g * (1.0 - s))).astype(BF)
                grads[pl.ds(to, 128), hidden + t:hidden + t + 128] = (h * a).astype(BF)
            return carry

        lax.fori_loop(0, 4, act, 0)

        @pl.when(q >= 2)
        def _():
            pair_copy(q - 2).wait_send()

        mine = grads[pl.ds(pl.multiple_of(ya * 512, 512), 512), :]
        for t in range(0, half, 512):
            w = wgu[pl.ds(pl.multiple_of((1 - c) * half + t, 512), 512), :]
            psend[q % 2, :, :, :, t:t + 512] = dot(mine, w, 1, 1).astype(BF).reshape(4, 4, CAP, 512)
        pair_copy(q).start()
        for t in range(0, half, 512):
            w = wgu[pl.ds(pl.multiple_of(c * half + t, 512), 512), :]
            own[:, t:t + 512] = dot(mine, w, 1, 1)
        pair_copy(q).wait_recv()
        for i in range(4):
            for t in range(0, half, 512):
                both = own[i * 128:(i + 1) * 128, t:t + 512].reshape(4, CAP, 512) + precv[q, i, :, :, t:t + 512].astype(F32)
                precv[q, i, :, :, t:t + 512] = both.astype(BF)
        for dz in range(4):
            @pl.when((q != 0) | (dz != 0))
            def _():
                back_copy(q, dz).start()

        @pl.when(q == 0)
        def _():
            back[e] = precv[0, z]

    def finish(r):
        home = chip(r // 4, gray(r % 4))
        for d in (1, 2, 3):
            x_landed(r, home, d).wait_recv()
        forward(r, home, c).start()

    def produce(r):
        dy, dz = r // 4, gray(r % 4)
        home = chip(dy, dz)

        @pl.when((r >= 1) & (r <= 3))
        def _():
            ay, az = axis_a(gray(r % 4))
            wait_block(ay, az)
            for i, d in enumerate((1, 3, 2)):
                ty, tz = axis_b(d)
                for cp in block_copies(ag.at[chip(ay, az)], mag.at[chip(ay, az)], ay, az, ty, tz, 3 + r * 3 + i):
                    cp.start()

        @pl.when(jnp.where(first, dy, dz) != 0)
        def _():
            wait_block(dy, dz)

        @pl.when(r >= SLOTS)
        def _():
            for d in (1, 2, 3):
                x_copy(r - SLOTS, home, d).wait_send()

        pick(r, home)
        for d in (1, 3, 2):
            x_copy(r, home, d).start()
        rows[c, home, x] = stage[r % SLOTS, x]

    def step(s, carry):
        @pl.when(s < 16)
        def _():
            produce(s)

        @pl.when((s >= LAG) & (s < 16 + LAG))
        def _():
            finish(s - LAG)

        @pl.when((s > LAG) & ((s - LAG) % 4 == 0))
        def _():
            chunk((s - LAG) // 4 - 1)
        return carry

    lax.fori_loop(0, 17 + LAG, step, 0)

    for d in (1, 2, 3):
        rank_landed(d).wait_recv()
    for k in range(4):
        m = xrank[k].astype(F32)
        for g in range(16):
            place[k, g * CAP:(g + 1) * CAP, :] = jnp.where(slot_ids == m[g:g + 1], 1.0, 0.0).astype(BF)

    def grad_out(t):
        at = pl.ds(pl.multiple_of(t * 512, 512), 512)
        return (pltpu.make_async_copy(gtile.at[t % 2, :, pl.ds(0, hidden)], og_ref.at[0, at, :], og_s.at[0, t]),
                pltpu.make_async_copy(gtile.at[t % 2, :, pl.ds(hidden, hidden)], ou_ref.at[0, at, :], og_s.at[1, t]),
                pltpu.make_async_copy(dtile.at[t % 2], od_ref.at[0, :, at], od_s.at[t]))

    for t in range(4):
        cols = slice(t * 512, (t + 1) * 512)
        if t >= 2:
            for cp in grad_out(t - 2):
                cp.wait()
        gtile[t % 2] = dot(rows[0, :, :, :, cols].reshape(2048, 512), grads[...], 0, 0).astype(BF)
        dtile[t % 2] = dot(hid[...], rows[1, :, :, :, cols].reshape(2048, 512), 0, 0).astype(BF)
        for cp in grad_out(t):
            cp.start()

    def waits(rel, carry):
        back_landed(rel // 4, rel % 4).wait_recv()
        return carry

    lax.fori_loop(1, 16, waits, 0)

    def combine(k, t):
        return dot(place[k], back[:, pl.ds(k, 1), :, t:t + 512].reshape(512, 512), 0, 0)

    def sum_copy(d):
        return remote(xsend.at[d - 1], xrecv.at[d - 1], t_s.at[d - 1], t_r.at[d - 1], (e, (x + d) % 4, c))

    for d in (2, 1, 3):
        for t in range(0, half, 512):
            xsend[d - 1, :, t:t + 512] = combine((x + d) % 4, t).astype(BF)
        sum_copy(d).start()
    for t in range(0, half, 512):
        own[0:128, t:t + 512] = combine(x, t)
    for d in (1, 3, 2):
        sum_copy(d).wait_recv()
    total = own[0:128, :]
    for d in (1, 2, 3):
        total = total + xrecv[d - 1].astype(F32)
    tok_ref[...] = total.astype(BF)

    def close(r, carry):
        home = chip(r // 4, gray(r % 4))
        forward(r, home, c).wait_send()

        @pl.when(r >= 16 - SLOTS)
        def _():
            for d in (1, 2, 3):
                x_copy(r, home, d).wait_send()

        @pl.when(r >= 1)
        def _():
            back_copy(r // 4, r % 4).wait_send()
        return carry

    lax.fori_loop(0, 16, close, 0)
    for slot in range(15):
        for cp in block_copies(src_ref, meta_ref, 0, 0, 0, 1, slot):
            cp.wait_send()
    for d in (1, 2, 3):
        rank_copy(d).wait_send()
        sum_copy(d).wait_send()
    for q in (2, 3):
        pair_copy(q).wait_send()
    for t in (2, 3):
        for cp in grad_out(t):
            cp.wait()


def layer(src, meta, ranks, w_gate, w_up, w_down):
    width = src.shape[1]
    hidden = w_gate.shape[2]
    half = width // 2
    dma = pltpu.SemaphoreType.DMA
    vmem = pl.BlockSpec(memory_space=pltpu.VMEM)
    hbm = pl.BlockSpec(memory_space=pl.ANY)
    return pl.pallas_call(
        layer_kernel,
        out_shape=(
            jax.ShapeDtypeStruct((128, half), BF),
            jax.ShapeDtypeStruct((1, width, hidden), BF),
            jax.ShapeDtypeStruct((1, width, hidden), BF),
            jax.ShapeDtypeStruct((1, hidden, width), BF),
        ),
        in_specs=[vmem, vmem, vmem, hbm, hbm, hbm],
        out_specs=(vmem, hbm, hbm, hbm),
        scratch_shapes=[
            pltpu.VMEM((16, 128, width), BF),
            pltpu.VMEM((16, 16, 16, 128), BF),
            pltpu.VMEM((SLOTS, 4, CAP, width), BF),
            pltpu.VMEM((2, 16, 4, CAP, width), BF),
            pltpu.VMEM((width, 2 * hidden), BF),
            pltpu.VMEM((hidden, width), BF),
            pltpu.VMEM((2048, hidden), BF),
            pltpu.VMEM((2048, 2 * hidden), BF),
            pltpu.VMEM((512, 2 * hidden), F32),
            pltpu.VMEM((512, hidden), F32),
            pltpu.VMEM((2, 4, 4, CAP, half), BF),
            pltpu.VMEM((4, 4, 4, CAP, half), BF),
            pltpu.VMEM((512, half), F32),
            pltpu.VMEM((16, 4, CAP, half), BF),
            pltpu.VMEM((4, 16, 128), BF),
            pltpu.VMEM((4, 512, 128), BF),
            pltpu.VMEM((3, 128, half), BF),
            pltpu.VMEM((3, 128, half), BF),
            pltpu.VMEM((2, 512, 2 * hidden), BF),
            pltpu.VMEM((2, hidden, 512), BF),
            dma((15,)), dma((16,)), dma((15,)), dma((16,)), dma((48,)), dma((48,)), dma((16,)), dma((16,)),
            dma((4,)), dma((4,)), dma((16,)), dma((16,)), dma((3,)), dma((3,)), dma((3,)), dma((3,)),
            dma((3,)), dma((2, 4)), dma((4,)),
        ],
        compiler_params=pltpu.CompilerParams(collective_id=0, has_side_effects=True, vmem_limit_bytes=67043328),
    )(src, meta, ranks, w_gate, w_up, w_down)


def routing(routes, gates):
    ids = jnp.arange(64, dtype=jnp.int32)
    hit = ids[:, None, None] == routes.T[None]
    mask = jnp.sum(hit.astype(F32), axis=1)
    gmap = jnp.sum(jnp.where(hit, gates.T[None], 0.0), axis=1)
    before = jnp.triu(jnp.ones((128, 128), BF), 1)
    rank = jnp.dot(mask.astype(BF), before, preferred_element_type=F32)
    rank = jnp.where(mask > 0, rank, 64.0)
    high = lax.reduce_precision(gmap, 8, 7)
    rest = gmap - high
    mid = lax.reduce_precision(rest, 8, 7)
    low = rest - mid
    return jnp.stack([rank, high, mid, low]).astype(BF)


def body(tokens, cotangent, routes, gates, gate_weight, up_weight, down_weight):
    c = lax.axis_index("tensor")
    maps = routing(routes, gates).reshape(4, 16, 4, 128)
    meta = maps.transpose(1, 0, 2, 3).reshape(16, 16, 128)
    ranks = maps[0].transpose(1, 0, 2)
    src = jnp.where(c == 0, tokens, cotangent)
    return layer(src, meta, ranks, gate_weight, up_weight, down_weight)


def solution(mesh):
    in_specs = (
        P(("expert", "replica"), None),
        P(("expert", "replica"), None),
        P(("expert", "replica"), None),
        P(("expert", "replica"), None),
        P("expert", None, "tensor"),
        P("expert", None, "tensor"),
        P("expert", "tensor", None),
    )
    out_specs = (
        P(("expert", "replica"), "tensor"),
        P(("expert", "replica"), None, "tensor"),
        P(("expert", "replica"), None, "tensor"),
        P(("expert", "replica"), "tensor", None),
    )
    return jax.shard_map(body, mesh=mesh, in_specs=in_specs, out_specs=out_specs, check_vma=False)
```

```python
import jax
import jax.numpy as jnp
from jax import lax
from jax.experimental import pallas as pl
from jax.experimental.pallas import tpu as pltpu
from jax.sharding import PartitionSpec as P

MESH = pl.DeviceIdType.MESH
CAP = 32
BF = jnp.bfloat16
F32 = jnp.float32
LAG = 4
SLOTS = 8
ORDER = ((0, 0), (0, 1), (1, 0), (0, 2), (2, 0), (1, 1), (3, 3), (2, 1),
         (1, 2), (3, 2), (2, 3), (2, 2), (1, 3), (3, 1), (0, 3), (3, 0))
EARLY = 14


def entry(r, column):
    if isinstance(r, int):
        return ORDER[r][column]
    found = 0
    for k, pair in enumerate(ORDER):
        if pair[column]:
            found = found + jnp.where(r == k, pair[column], 0)
    return found


def offset(r):
    return entry(r, 0), entry(r, 1)


def dot(a, b, ca, cb):
    return lax.dot_general(a, b, (((ca,), (cb,)), ((), ())), preferred_element_type=F32)


def layer_kernel(token_ref, cot_ref, meta_ref, rank_ref, wg_ref, wu_ref, wd_ref,
                 tok_ref, og_ref, ou_ref, od_ref,
                 ag, mag, stage, rows, wgu, wd, hid, grads, gu, hg, psend, precv, own, back,
                 last, xrank, place, lplace, xsend, xrecv, gtile, dtile,
                 ag_s, ag_r, mg_s, mg_r, x_s, x_r, f_s, f_r, p_s, p_r, b_s, b_r, l_s, l_r, k_s, k_r, t_s, t_r, w_s, og_s, od_s, i_s):
    e = lax.axis_index("expert")
    x = lax.axis_index("replica")
    c = lax.axis_index("tensor")
    y, z = e // 4, e % 4
    first = c == 0
    width = token_ref.shape[1]
    half = width // 2
    hidden = wd.shape[0]

    def chip(dy, dz):
        return ((y + dy + 4) % 4) * 4 + (z + dz + 4) % 4

    def remote(src, dst, send, recv, dev):
        return pltpu.make_async_remote_copy(src_ref=src, dst_ref=dst, send_sem=send, recv_sem=recv,
                                            device_id=dev, device_id_type=MESH)

    def axis_a(d):
        return jnp.where(first, 0, d), jnp.where(first, d, 0)

    def axis_b(d):
        return jnp.where(first, d, 0), jnp.where(first, 0, d)

    partner = (e, x, 1 - c)

    def weights():
        return (pltpu.make_async_copy(wg_ref.at[x], wgu.at[:, pl.ds(0, hidden)], w_s.at[0]),
                pltpu.make_async_copy(wu_ref.at[x], wgu.at[:, pl.ds(hidden, hidden)], w_s.at[1]),
                pltpu.make_async_copy(wd_ref.at[x], wd, w_s.at[2]))

    @pl.when(first)
    def _():
        pltpu.make_async_copy(token_ref, ag.at[e], i_s).start()

    @pl.when(jnp.logical_not(first))
    def _():
        pltpu.make_async_copy(cot_ref, ag.at[e], i_s).start()

    barrier = pltpu.get_barrier_semaphore()
    for rel in range(1, 16):
        pl.semaphore_signal(barrier, inc=1, device_id=(chip(rel // 4, rel % 4), x, c), device_id_type=MESH)
    for d in (1, 2, 3):
        pl.semaphore_signal(barrier, inc=1, device_id=(e, (x + d) % 4, c), device_id_type=MESH)
        for r in (14, 15):
            dy, dz = ORDER[r]
            pl.semaphore_signal(barrier, inc=1, device_id=(chip(dy, dz), (x + d) % 4, c), device_id_type=MESH)
            pl.semaphore_signal(barrier, inc=1, device_id=(chip(-dy, -dz), (x + d) % 4, c), device_id_type=MESH)
    pl.semaphore_signal(barrier, inc=1, device_id=partner, device_id_type=MESH)
    pltpu.make_async_copy(token_ref, ag.at[e], i_s).wait()
    pl.semaphore_wait(barrier, 31)

    def block_copies(src, msrc, by, bz, ty, tz, slot):
        home = chip(by, bz)
        landed = ((by - ty + 4) % 4) * 4 + (bz - tz + 4) % 4
        dev = (chip(ty, tz), x, c)
        return (remote(msrc, mag.at[home], mg_s.at[slot], mg_r.at[landed], dev),
                remote(src, ag.at[home], ag_s.at[slot], ag_r.at[landed], dev))

    def wait_block(by, bz):
        rel, home = by * 4 + bz, chip(by, bz)
        remote(meta_ref, mag.at[home], mg_s.at[0], mg_r.at[rel], partner).wait_recv()
        remote(ag.at[e], ag.at[home], ag_s.at[0], ag_r.at[rel], partner).wait_recv()

    for i, d in enumerate((1, 3, 2)):
        for ax, base in ((axis_a, 0), (axis_b, 3)):
            ty, tz = ax(d)
            for cp in block_copies(ag.at[e], meta_ref, 0, 0, ty, tz, base + i):
                cp.start()

    def rank_copy(d):
        return remote(rank_ref.at[(x + d) % 4], xrank.at[x], k_s.at[d - 1], k_r.at[d - 1], (e, (x + d) % 4, c))

    def rank_landed(d):
        return remote(rank_ref.at[0], xrank.at[(x - d + 4) % 4], k_s.at[d - 1], k_r.at[d - 1], partner)

    for d in (1, 2, 3):
        rank_copy(d).start()
    xrank[x] = rank_ref[x]
    mag[e] = meta_ref[...]
    for cp in weights():
        cp.start()

    def x_copy(r, d):
        return remote(stage.at[r % SLOTS, (x + d) % 4], rows.at[c, r, x], x_s.at[r * 3 + d - 1],
                      x_r.at[r * 3 + d - 1], (e, (x + d) % 4, c))

    def x_landed(r, d):
        return remote(stage.at[0, 0], rows.at[c, r, (x - d + 4) % 4], x_s.at[r * 3 + d - 1],
                      x_r.at[r * 3 + d - 1], partner)

    def forward(r, kind):
        return remote(rows.at[kind, r], rows.at[kind, r], f_s.at[r], f_r.at[r], partner)

    slot_ids = lax.broadcasted_iota(jnp.int32, (CAP, 128), 0).astype(F32)

    def pick(r, home):
        m = mag[home, e].astype(F32)
        gsum = m[4:8] + m[8:12] + m[12:16]
        sel, scale = [], []
        for j in range(4):
            s = jnp.where(slot_ids == m[j:j + 1], 1.0, 0.0)
            sel.append(s)
            scale.append(jnp.sum(s * gsum[j:j + 1], axis=1, keepdims=True))
        sel = jnp.concatenate(sel, axis=0).astype(BF)
        scale = jnp.concatenate(scale, axis=0)
        scale = jnp.where(first, jnp.ones_like(scale), scale)
        for t in range(0, width, 512):
            got = dot(sel, ag[home, :, t:t + 512], 1, 0) * scale
            stage[r % SLOTS, :, :, t:t + 512] = got.astype(BF).reshape(4, CAP, 512)

    def pair_copy(q):
        return remote(psend.at[q % 2], precv.at[q], p_s.at[q], p_r.at[q], partner)

    def back_copy(r):
        dy, dz = offset(r)
        return remote(precv.at[r // 2, r % 2], back.at[r], b_s.at[r], b_r.at[r], (chip(dy, dz), x, c))

    def last_copy(i, d):
        dy, dz = ORDER[EARLY + i]
        return remote(precv.at[7, i, (x + d) % 4], last.at[i, x], l_s.at[i, d], l_r.at[i, d],
                      (chip(dy, dz), (x + d) % 4, c))

    def last_landed(i, d):
        return remote(precv.at[7, i, 0], last.at[i, (x - d + 4) % 4], l_s.at[i, d], l_r.at[i, d], partner)

    def chunk(q):
        for i in range(2):
            forward(q * 2 + i, 1 - c).wait_recv()

        @pl.when(q == 0)
        def _():
            for cp in weights():
                cp.wait()

        gu[...] = dot(rows[0, pl.ds(q * 2, 2)].reshape(256, width), wgu[...], 1, 0)
        hg[...] = dot(rows[1, pl.ds(q * 2, 2)].reshape(256, width), wd[...], 1, 1)

        def act(i, carry):
            at = pl.multiple_of(i * 128, 128)
            to = pl.multiple_of(q * 256 + i * 128, 128)
            for t in range(0, hidden, 128):
                g = gu[pl.ds(at, 128), t:t + 128]
                u = gu[pl.ds(at, 128), hidden + t:hidden + t + 128]
                h = hg[pl.ds(at, 128), t:t + 128]
                s = jax.nn.sigmoid(g)
                a = g * s
                hid[pl.ds(to, 128), t:t + 128] = (a * u).astype(BF)
                grads[pl.ds(to, 128), t:t + 128] = (h * u * s * (1.0 + g * (1.0 - s))).astype(BF)
                grads[pl.ds(to, 128), hidden + t:hidden + t + 128] = (h * a).astype(BF)
            return carry

        lax.fori_loop(0, 2, act, 0)

        @pl.when(q >= 2)
        def _():
            pair_copy(q - 2).wait_send()

        mine = grads[pl.ds(pl.multiple_of(q * 256, 256), 256), :]
        for t in range(0, half, 512):
            w = wgu[pl.ds(pl.multiple_of((1 - c) * half + t, 512), 512), :]
            psend[q % 2, :, :, :, t:t + 512] = dot(mine, w, 1, 1).astype(BF).reshape(2, 4, CAP, 512)
        pair_copy(q).start()
        for t in range(0, half, 512):
            w = wgu[pl.ds(pl.multiple_of(c * half + t, 512), 512), :]
            own[:, t:t + 512] = dot(mine, w, 1, 1)
        pair_copy(q).wait_recv()
        for i in range(2):
            for t in range(0, half, 512):
                both = own[i * 128:(i + 1) * 128, t:t + 512].reshape(4, CAP, 512) + precv[q, i, :, :, t:t + 512].astype(F32)
                precv[q, i, :, :, t:t + 512] = both.astype(BF)
        for i in range(2):
            @pl.when((q < 7) & (q + i > 0))
            def _():
                back_copy(q * 2 + i).start()

        @pl.when(q == 0)
        def _():
            back[0] = precv[0, 0]

        @pl.when(q == 7)
        def _():
            for d in (2, 1, 3, 0):
                for i in range(2):
                    last_copy(i, d).start()

    def finish(r):
        for d in (1, 2, 3):
            x_landed(r, d).wait_recv()
        forward(r, c).start()

    def produce(r):
        dy, dz = offset(r)

        def spread(d, base):
            ay, az = axis_a(d)
            wait_block(ay, az)
            at = chip(ay, az)
            for i, far in enumerate((1, 3, 2)):
                ty, tz = axis_b(far)
                for cp in block_copies(ag.at[at], mag.at[at], ay, az, ty, tz, base + i):
                    cp.start()

        @pl.when(r == 1)
        def _():
            spread(1, 6)
            spread(3, 9)

        @pl.when(r == 3)
        def _():
            spread(2, 12)

        @pl.when(jnp.where(first, dy, dz) != 0)
        def _():
            wait_block(dy, dz)

        @pl.when(r >= SLOTS)
        def _():
            for d in (1, 2, 3):
                x_copy(r - SLOTS, d).wait_send()

        pick(r, chip(dy, dz))
        for d in (1, 3, 2):
            x_copy(r, d).start()
        rows[c, r, x] = stage[r % SLOTS, x]

    def combine(k, t):
        return dot(place[k], back[:, pl.ds(k, 1), :, t:t + 512].reshape(EARLY * CAP, 512), 0, 0)

    def sum_copy(d):
        return remote(xsend.at[d - 1], xrecv.at[d - 1], t_s.at[d - 1], t_r.at[d - 1], (e, (x + d) % 4, c))

    def places():
        for d in (1, 2, 3):
            rank_landed(d).wait_recv()
        for r in range(EARLY):
            dy, dz = ORDER[r]
            for k in range(4):
                m = xrank[k, pl.ds(chip(-dy, -dz), 1), :]
                place[k, r * CAP:(r + 1) * CAP, :] = jnp.where(slot_ids == m, 1.0, 0.0).astype(BF)
        for i in range(2):
            dy, dz = ORDER[EARLY + i]
            for k in range(4):
                m = rank_ref[k, pl.ds(chip(-dy, -dz), 1), :]
                lplace[(i * 4 + k) * CAP:(i * 4 + k + 1) * CAP, :] = jnp.where(slot_ids == m, 1.0, 0.0).astype(BF)

    def early_sums():
        def waits(r, carry):
            back_copy(r).wait_recv()
            return carry

        lax.fori_loop(1, EARLY, waits, 0)
        for d in (2, 1, 3):
            for t in range(0, half, 512):
                xsend[d - 1, :, t:t + 512] = combine((x + d) % 4, t).astype(BF)
            sum_copy(d).start()

    def step(s, carry):
        @pl.when(s < 16)
        def _():
            produce(s)

        @pl.when((s >= LAG) & (s < 16 + LAG))
        def _():
            finish(s - LAG)

        @pl.when(s == 9)
        def _():
            places()

        @pl.when(s == 16 + LAG)
        def _():
            early_sums()

        @pl.when((s > LAG) & ((s - LAG) % 2 == 0))
        def _():
            chunk((s - LAG) // 2 - 1)
        return carry

    lax.fori_loop(0, 17 + LAG, step, 0)

    def grad_out(t):
        at = pl.ds(pl.multiple_of(t * 512, 512), 512)
        return (pltpu.make_async_copy(gtile.at[t % 2, :, pl.ds(0, hidden)], og_ref.at[0, at, :], og_s.at[0, t]),
                pltpu.make_async_copy(gtile.at[t % 2, :, pl.ds(hidden, hidden)], ou_ref.at[0, at, :], og_s.at[1, t]),
                pltpu.make_async_copy(dtile.at[t % 2], od_ref.at[0, :, at], od_s.at[t]))

    for t in range(4):
        cols = slice(t * 512, (t + 1) * 512)
        if t >= 2:
            for cp in grad_out(t - 2):
                cp.wait()
        gtile[t % 2] = dot(rows[0, :, :, :, cols].reshape(2048, 512), grads[...], 0, 0).astype(BF)
        dtile[t % 2] = dot(hid[...], rows[1, :, :, :, cols].reshape(2048, 512), 0, 0).astype(BF)
        for cp in grad_out(t):
            cp.start()

    for t in range(0, half, 512):
        own[0:128, t:t + 512] = combine(x, t)
    for d in (1, 3, 2):
        sum_copy(d).wait_recv()
        own[0:128, :] = own[0:128, :] + xrecv[d - 1].astype(F32)
    for i in range(2):
        for d in range(4):
            last_landed(i, d).wait_recv()
    for t in range(0, half, 512):
        got = dot(lplace[...], last[:, :, :, t:t + 512].reshape(8 * CAP, 512), 0, 0)
        tok_ref[:, t:t + 512] = (own[0:128, t:t + 512] + got).astype(BF)

    def close(r, carry):
        forward(r, c).wait_send()

        @pl.when(r >= 16 - SLOTS)
        def _():
            for d in (1, 2, 3):
                x_copy(r, d).wait_send()

        @pl.when((r >= 1) & (r < EARLY))
        def _():
            back_copy(r).wait_send()
        return carry

    lax.fori_loop(0, 16, close, 0)
    for i in range(2):
        for d in range(4):
            last_copy(i, d).wait_send()
    for slot in range(15):
        for cp in block_copies(ag.at[e], meta_ref, 0, 0, 0, 1, slot):
            cp.wait_send()
    for d in (1, 2, 3):
        rank_copy(d).wait_send()
        sum_copy(d).wait_send()
    for q in (6, 7):
        pair_copy(q).wait_send()
    for t in (2, 3):
        for cp in grad_out(t):
            cp.wait()


def layer(tokens, cotangent, meta, ranks, w_gate, w_up, w_down):
    width = tokens.shape[1]
    hidden = w_gate.shape[2]
    half = width // 2
    dma = pltpu.SemaphoreType.DMA
    vmem = pl.BlockSpec(memory_space=pltpu.VMEM)
    hbm = pl.BlockSpec(memory_space=pl.ANY)
    return pl.pallas_call(
        layer_kernel,
        out_shape=(
            jax.ShapeDtypeStruct((128, half), BF),
            jax.ShapeDtypeStruct((1, width, hidden), BF),
            jax.ShapeDtypeStruct((1, width, hidden), BF),
            jax.ShapeDtypeStruct((1, hidden, width), BF),
        ),
        in_specs=[hbm, hbm, vmem, vmem, hbm, hbm, hbm],
        out_specs=(vmem, hbm, hbm, hbm),
        scratch_shapes=[
            pltpu.VMEM((16, 128, width), BF),
            pltpu.VMEM((16, 16, 16, 128), BF),
            pltpu.VMEM((SLOTS, 4, CAP, width), BF),
            pltpu.VMEM((2, 16, 4, CAP, width), BF),
            pltpu.VMEM((width, 2 * hidden), BF),
            pltpu.VMEM((hidden, width), BF),
            pltpu.VMEM((2048, hidden), BF),
            pltpu.VMEM((2048, 2 * hidden), BF),
            pltpu.VMEM((256, 2 * hidden), F32),
            pltpu.VMEM((256, hidden), F32),
            pltpu.VMEM((2, 2, 4, CAP, half), BF),
            pltpu.VMEM((8, 2, 4, CAP, half), BF),
            pltpu.VMEM((256, half), F32),
            pltpu.VMEM((EARLY, 4, CAP, half), BF),
            pltpu.VMEM((2, 4, CAP, half), BF),
            pltpu.VMEM((4, 16, 128), F32),
            pltpu.VMEM((4, EARLY * CAP, 128), BF),
            pltpu.VMEM((8 * CAP, 128), BF),
            pltpu.VMEM((3, 128, half), BF),
            pltpu.VMEM((3, 128, half), BF),
            pltpu.VMEM((2, 512, 2 * hidden), BF),
            pltpu.VMEM((2, hidden, 512), BF),
            dma((15,)), dma((16,)), dma((15,)), dma((16,)), dma((48,)), dma((48,)), dma((16,)), dma((16,)),
            dma((8,)), dma((8,)), dma((EARLY,)), dma((EARLY,)), dma((2, 4)), dma((2, 4)),
            dma((3,)), dma((3,)), dma((3,)), dma((3,)), dma((3,)), dma((2, 4)), dma((4,)), pltpu.SemaphoreType.DMA,
        ],
        compiler_params=pltpu.CompilerParams(collective_id=0, has_side_effects=True, vmem_limit_bytes=67043328),
    )(tokens, cotangent, meta, ranks, w_gate, w_up, w_down)


def routing(routes, gates):
    ids = jnp.arange(64, dtype=jnp.int32)
    hit = ids[:, None, None] == routes.T[None]
    mask = jnp.sum(hit.astype(F32), axis=1)
    gmap = jnp.sum(jnp.where(hit, gates.T[None], 0.0), axis=1)
    before = jnp.triu(jnp.ones((128, 128), BF), 1)
    rank = jnp.dot(mask.astype(BF), before, preferred_element_type=F32)
    rank = jnp.where(mask > 0, rank, 64.0)
    high = lax.reduce_precision(gmap, 8, 7)
    rest = gmap - high
    mid = lax.reduce_precision(rest, 8, 7)
    low = rest - mid
    return rank, jnp.stack([rank, high, mid, low]).astype(BF)


def body(tokens, cotangent, routes, gates, gate_weight, up_weight, down_weight):
    rank, maps = routing(routes, gates)
    meta = maps.reshape(4, 16, 4, 128).transpose(1, 0, 2, 3).reshape(16, 16, 128)
    ranks = rank.reshape(16, 4, 128).transpose(1, 0, 2)
    return layer(tokens, cotangent, meta, ranks, gate_weight, up_weight, down_weight)


def solution(mesh):
    in_specs = (
        P(("expert", "replica"), None),
        P(("expert", "replica"), None),
        P(("expert", "replica"), None),
        P(("expert", "replica"), None),
        P("expert", None, "tensor"),
        P("expert", None, "tensor"),
        P("expert", "tensor", None),
    )
    out_specs = (
        P(("expert", "replica"), "tensor"),
        P(("expert", "replica"), None, "tensor"),
        P(("expert", "replica"), None, "tensor"),
        P(("expert", "replica"), "tensor", None),
    )
    return jax.shard_map(body, mesh=mesh, in_specs=in_specs, out_specs=out_specs, check_vma=False)
```

```python
import jax
import jax.numpy as jnp
from jax import lax
from jax.experimental import pallas as pl
from jax.experimental.pallas import tpu as pltpu
from jax.sharding import PartitionSpec as P

MESH = pl.DeviceIdType.MESH
CAP = 32
BF = jnp.bfloat16
F32 = jnp.float32
LAG = 4
SLOTS = 8
ORDER = ((0, 0), (0, 1), (1, 0), (0, 2), (2, 0), (1, 1), (3, 3), (2, 1),
         (1, 2), (3, 2), (2, 3), (2, 2), (1, 3), (3, 1), (0, 3), (3, 0))
EARLY = 14


def entry(r, column):
    if isinstance(r, int):
        return ORDER[r][column]
    found = 0
    for k, pair in enumerate(ORDER):
        if pair[column]:
            found = found + jnp.where(r == k, pair[column], 0)
    return found


def offset(r):
    return entry(r, 0), entry(r, 1)


def dot(a, b, ca, cb):
    return lax.dot_general(a, b, (((ca,), (cb,)), ((), ())), preferred_element_type=F32)


def layer_kernel(token_ref, cot_ref, meta_ref, rank_ref, wg_ref, wu_ref, wd_ref,
                 tok_ref, og_ref, ou_ref, od_ref,
                 ag, mag, stage, rows, wgu, wd, hid, grads, gu, hg, psend, precv, own, back,
                 last, xrank, place, lplace, xsend, xrecv, gtile, dtile,
                 ag_s, ag_r, mg_s, mg_r, x_s, x_r, f_s, f_r, p_s, p_r, b_s, b_r, l_s, l_r, k_s, k_r, t_s, t_r, w_s, og_s, od_s, i_s):
    e = lax.axis_index("expert")
    x = lax.axis_index("replica")
    c = lax.axis_index("tensor")
    y, z = e // 4, e % 4
    first = c == 0
    width = token_ref.shape[1]
    half = width // 2
    hidden = wd.shape[0]

    def chip(dy, dz):
        return ((y + dy + 4) % 4) * 4 + (z + dz + 4) % 4

    def remote(src, dst, send, recv, dev):
        return pltpu.make_async_remote_copy(src_ref=src, dst_ref=dst, send_sem=send, recv_sem=recv,
                                            device_id=dev, device_id_type=MESH)

    def at(a, b):
        return jnp.where(first, b, a), jnp.where(first, a, b)

    partner = (e, x, 1 - c)

    def weights():
        return (pltpu.make_async_copy(wg_ref.at[x], wgu.at[:, pl.ds(0, hidden)], w_s.at[0]),
                pltpu.make_async_copy(wu_ref.at[x], wgu.at[:, pl.ds(hidden, hidden)], w_s.at[1]),
                pltpu.make_async_copy(wd_ref.at[x], wd, w_s.at[2]))

    @pl.when(first)
    def _():
        pltpu.make_async_copy(token_ref, ag.at[e], i_s).start()

    @pl.when(jnp.logical_not(first))
    def _():
        pltpu.make_async_copy(cot_ref, ag.at[e], i_s).start()

    barrier = pltpu.get_barrier_semaphore()
    for rel in range(1, 16):
        pl.semaphore_signal(barrier, inc=1, device_id=(chip(rel // 4, rel % 4), x, c), device_id_type=MESH)
    for d in (1, 2, 3):
        pl.semaphore_signal(barrier, inc=1, device_id=(e, (x + d) % 4, c), device_id_type=MESH)
        for r in (14, 15):
            dy, dz = ORDER[r]
            pl.semaphore_signal(barrier, inc=1, device_id=(chip(dy, dz), (x + d) % 4, c), device_id_type=MESH)
            pl.semaphore_signal(barrier, inc=1, device_id=(chip(-dy, -dz), (x + d) % 4, c), device_id_type=MESH)
    pl.semaphore_signal(barrier, inc=1, device_id=partner, device_id_type=MESH)
    pltpu.make_async_copy(token_ref, ag.at[e], i_s).wait()
    pl.semaphore_wait(barrier, 31)

    def meta_copy(rel):
        dy, dz = rel // 4, rel % 4
        target = chip(dy, dz)
        landed = ((4 - dy) % 4) * 4 + (4 - dz) % 4
        return remote(meta_ref.at[target], mag.at[e], mg_s.at[rel], mg_r.at[landed], (target, x, c))

    def block_copy(a, b, da, db, slot, part=None):
        by, bz = at(a, b)
        ty, tz = at(da, db)
        home = chip(by, bz)
        landed = ((by - ty + 4) % 4) * 4 + (bz - tz + 4) % 4
        if part is None:
            piece, recv = ag.at[home], ag_r.at[landed, 0]
        else:
            piece, recv = ag.at[home, pl.ds(part * 64, 64)], ag_r.at[landed, part]
        return remote(piece, piece, ag_s.at[slot], recv, (chip(ty, tz), x, c))

    def wait_block(a, b, parts=False):
        by, bz = at(a, b)
        rel, home = by * 4 + bz, chip(by, bz)
        if parts:
            for part in range(2):
                piece = ag.at[home, pl.ds(part * 64, 64)]
                remote(piece, piece, ag_s.at[0], ag_r.at[rel, part], partner).wait_recv()
        else:
            remote(ag.at[home], ag.at[home], ag_s.at[0], ag_r.at[rel, 0], partner).wait_recv()

    def relay(a, slot):
        wait_block(a, 1)
        block_copy(a, 1, 0, 3, slot, 0).start()
        wait_block(a, 3)
        block_copy(a, 3, 0, 1, slot + 1, 1).start()

    def gather(s):
        @pl.when(s == 1)
        def _():
            wait_block(1, 0)
            block_copy(1, 0, 3, 0, 4, 0).start()
            wait_block(3, 0)
            block_copy(3, 0, 1, 0, 5, 1).start()
            block_copy(1, 0, 0, 1, 6).start()
            block_copy(1, 0, 0, 3, 7).start()
            block_copy(3, 0, 0, 1, 8).start()
            block_copy(3, 0, 0, 3, 9).start()
            relay(0, 12)
            for rel in range(1, 16):
                meta_copy(rel).wait_recv()

        @pl.when(s == 3)
        def _():
            wait_block(2, 0, True)
            block_copy(2, 0, 0, 1, 10).start()
            block_copy(2, 0, 0, 3, 11).start()

        @pl.when(s == 5)
        def _():
            relay(1, 14)
            relay(3, 16)

        @pl.when(s == 7)
        def _():
            relay(2, 18)

    for rel in range(1, 16):
        meta_copy(rel).start()
    for i, (da, db) in enumerate(((1, 0), (3, 0), (0, 1), (0, 3))):
        block_copy(0, 0, da, db, i).start()

    def rank_copy(d):
        return remote(rank_ref.at[(x + d) % 4], xrank.at[x], k_s.at[d - 1], k_r.at[d - 1], (e, (x + d) % 4, c))

    def rank_landed(d):
        return remote(rank_ref.at[0], xrank.at[(x - d + 4) % 4], k_s.at[d - 1], k_r.at[d - 1], partner)

    for d in (1, 2, 3):
        rank_copy(d).start()
    xrank[x] = rank_ref[x]
    mag[e] = meta_ref[e]
    for cp in weights():
        cp.start()

    def x_copy(r, d):
        return remote(stage.at[r % SLOTS, (x + d) % 4], rows.at[c, r, x], x_s.at[r * 3 + d - 1],
                      x_r.at[r * 3 + d - 1], (e, (x + d) % 4, c))

    def x_landed(r, d):
        return remote(stage.at[0, 0], rows.at[c, r, (x - d + 4) % 4], x_s.at[r * 3 + d - 1],
                      x_r.at[r * 3 + d - 1], partner)

    def forward(r, kind):
        return remote(rows.at[kind, r], rows.at[kind, r], f_s.at[r], f_r.at[r], partner)

    slot_ids = lax.broadcasted_iota(jnp.int32, (CAP, 128), 0).astype(F32)

    def pick(r, home):
        m = mag[home].astype(F32)
        gsum = m[4:8] + m[8:12] + m[12:16]
        sel, scale = [], []
        for j in range(4):
            s = jnp.where(slot_ids == m[j:j + 1], 1.0, 0.0)
            sel.append(s)
            scale.append(jnp.sum(s * gsum[j:j + 1], axis=1, keepdims=True))
        sel = jnp.concatenate(sel, axis=0).astype(BF)
        scale = jnp.concatenate(scale, axis=0)
        scale = jnp.where(first, jnp.ones_like(scale), scale)
        for t in range(0, width, 512):
            got = dot(sel, ag[home, :, t:t + 512], 1, 0) * scale
            stage[r % SLOTS, :, :, t:t + 512] = got.astype(BF).reshape(4, CAP, 512)

    def pair_copy(q):
        return remote(psend.at[q % 2], precv.at[q], p_s.at[q], p_r.at[q], partner)

    def back_copy(r):
        dy, dz = offset(r)
        return remote(precv.at[r // 2, r % 2], back.at[r], b_s.at[r], b_r.at[r], (chip(dy, dz), x, c))

    def last_copy(i, d):
        dy, dz = ORDER[EARLY + i]
        return remote(precv.at[7, i, (x + d) % 4], last.at[i, x], l_s.at[i, d], l_r.at[i, d],
                      (chip(dy, dz), (x + d) % 4, c))

    def last_landed(i, d):
        return remote(precv.at[7, i, 0], last.at[i, (x - d + 4) % 4], l_s.at[i, d], l_r.at[i, d], partner)

    def chunk(q):
        for i in range(2):
            forward(q * 2 + i, 1 - c).wait_recv()

        @pl.when(q == 0)
        def _():
            for cp in weights():
                cp.wait()

        gu[...] = dot(rows[0, pl.ds(q * 2, 2)].reshape(256, width), wgu[...], 1, 0)
        hg[...] = dot(rows[1, pl.ds(q * 2, 2)].reshape(256, width), wd[...], 1, 1)

        def act(i, carry):
            at = pl.multiple_of(i * 128, 128)
            to = pl.multiple_of(q * 256 + i * 128, 128)
            for t in range(0, hidden, 128):
                g = gu[pl.ds(at, 128), t:t + 128]
                u = gu[pl.ds(at, 128), hidden + t:hidden + t + 128]
                h = hg[pl.ds(at, 128), t:t + 128]
                s = jax.nn.sigmoid(g)
                a = g * s
                hid[pl.ds(to, 128), t:t + 128] = (a * u).astype(BF)
                grads[pl.ds(to, 128), t:t + 128] = (h * u * s * (1.0 + g * (1.0 - s))).astype(BF)
                grads[pl.ds(to, 128), hidden + t:hidden + t + 128] = (h * a).astype(BF)
            return carry

        lax.fori_loop(0, 2, act, 0)

        @pl.when(q >= 2)
        def _():
            pair_copy(q - 2).wait_send()

        mine = grads[pl.ds(pl.multiple_of(q * 256, 256), 256), :]
        for t in range(0, half, 512):
            w = wgu[pl.ds(pl.multiple_of((1 - c) * half + t, 512), 512), :]
            psend[q % 2, :, :, :, t:t + 512] = dot(mine, w, 1, 1).astype(BF).reshape(2, 4, CAP, 512)
        pair_copy(q).start()
        for t in range(0, half, 512):
            w = wgu[pl.ds(pl.multiple_of(c * half + t, 512), 512), :]
            own[:, t:t + 512] = dot(mine, w, 1, 1)
        pair_copy(q).wait_recv()
        for i in range(2):
            for t in range(0, half, 512):
                both = own[i * 128:(i + 1) * 128, t:t + 512].reshape(4, CAP, 512) + precv[q, i, :, :, t:t + 512].astype(F32)
                precv[q, i, :, :, t:t + 512] = both.astype(BF)
        for i in range(2):
            @pl.when((q < 7) & (q + i > 0))
            def _():
                back_copy(q * 2 + i).start()

        @pl.when(q == 0)
        def _():
            back[0] = precv[0, 0]

        @pl.when(q == 7)
        def _():
            for d in (2, 1, 3, 0):
                for i in range(2):
                    last_copy(i, d).start()

    def finish(r):
        for d in (1, 2, 3):
            x_landed(r, d).wait_recv()
        forward(r, c).start()

    def produce(r):
        dy, dz = offset(r)

        @pl.when(jnp.where(first, dy, dz) == 2)
        def _():
            wait_block(jnp.where(first, dz, dy), 2, True)

        @pl.when(r >= SLOTS)
        def _():
            for d in (1, 2, 3):
                x_copy(r - SLOTS, d).wait_send()

        pick(r, chip(dy, dz))
        for d in (1, 3, 2):
            x_copy(r, d).start()
        rows[c, r, x] = stage[r % SLOTS, x]

    def combine(k, t):
        return dot(place[k], back[:, pl.ds(k, 1), :, t:t + 512].reshape(EARLY * CAP, 512), 0, 0)

    def sum_copy(d):
        return remote(xsend.at[d - 1], xrecv.at[d - 1], t_s.at[d - 1], t_r.at[d - 1], (e, (x + d) % 4, c))

    def places():
        for d in (1, 2, 3):
            rank_landed(d).wait_recv()
        for r in range(EARLY):
            dy, dz = ORDER[r]
            for k in range(4):
                m = xrank[k, pl.ds(chip(-dy, -dz), 1), :]
                place[k, r * CAP:(r + 1) * CAP, :] = jnp.where(slot_ids == m, 1.0, 0.0).astype(BF)
        for i in range(2):
            dy, dz = ORDER[EARLY + i]
            for k in range(4):
                m = rank_ref[k, pl.ds(chip(-dy, -dz), 1), :]
                lplace[(i * 4 + k) * CAP:(i * 4 + k + 1) * CAP, :] = jnp.where(slot_ids == m, 1.0, 0.0).astype(BF)

    def early_sums():
        def waits(r, carry):
            back_copy(r).wait_recv()
            return carry

        lax.fori_loop(1, EARLY, waits, 0)
        for d in (2, 1, 3):
            for t in range(0, half, 512):
                xsend[d - 1, :, t:t + 512] = combine((x + d) % 4, t).astype(BF)
            sum_copy(d).start()

    def step(s, carry):
        @pl.when(s < 16)
        def _():
            gather(s)
            produce(s)

        @pl.when((s >= LAG) & (s < 16 + LAG))
        def _():
            finish(s - LAG)

        @pl.when(s == 9)
        def _():
            places()

        @pl.when(s == 16 + LAG)
        def _():
            early_sums()

        @pl.when((s > LAG) & ((s - LAG) % 2 == 0))
        def _():
            chunk((s - LAG) // 2 - 1)
        return carry

    lax.fori_loop(0, 17 + LAG, step, 0)

    def grad_out(t):
        at = pl.ds(pl.multiple_of(t * 512, 512), 512)
        return (pltpu.make_async_copy(gtile.at[t % 2, :, pl.ds(0, hidden)], og_ref.at[0, at, :], og_s.at[0, t]),
                pltpu.make_async_copy(gtile.at[t % 2, :, pl.ds(hidden, hidden)], ou_ref.at[0, at, :], og_s.at[1, t]),
                pltpu.make_async_copy(dtile.at[t % 2], od_ref.at[0, :, at], od_s.at[t]))

    for t in range(4):
        cols = slice(t * 512, (t + 1) * 512)
        if t >= 2:
            for cp in grad_out(t - 2):
                cp.wait()
        gtile[t % 2] = dot(rows[0, :, :, :, cols].reshape(2048, 512), grads[...], 0, 0).astype(BF)
        dtile[t % 2] = dot(hid[...], rows[1, :, :, :, cols].reshape(2048, 512), 0, 0).astype(BF)
        for cp in grad_out(t):
            cp.start()

    for t in range(0, half, 512):
        own[0:128, t:t + 512] = combine(x, t)
    for d in (1, 3, 2):
        sum_copy(d).wait_recv()
        own[0:128, :] = own[0:128, :] + xrecv[d - 1].astype(F32)
    for i in range(2):
        for d in range(4):
            last_landed(i, d).wait_recv()
    for t in range(0, half, 512):
        got = dot(lplace[...], last[:, :, :, t:t + 512].reshape(8 * CAP, 512), 0, 0)
        tok_ref[:, t:t + 512] = (own[0:128, t:t + 512] + got).astype(BF)

    def close(r, carry):
        forward(r, c).wait_send()

        @pl.when(r >= 16 - SLOTS)
        def _():
            for d in (1, 2, 3):
                x_copy(r, d).wait_send()

        @pl.when((r >= 1) & (r < EARLY))
        def _():
            back_copy(r).wait_send()
        return carry

    lax.fori_loop(0, 16, close, 0)
    for i in range(2):
        for d in range(4):
            last_copy(i, d).wait_send()
    for slot in range(20):
        half_sent = slot in (4, 5) or slot >= 12
        block_copy(0, 0, 1, 0, slot, 0 if half_sent else None).wait_send()
    for rel in range(1, 16):
        meta_copy(rel).wait_send()
    for d in (1, 2, 3):
        rank_copy(d).wait_send()
        sum_copy(d).wait_send()
    for q in (6, 7):
        pair_copy(q).wait_send()
    for t in (2, 3):
        for cp in grad_out(t):
            cp.wait()


def layer(tokens, cotangent, meta, ranks, w_gate, w_up, w_down):
    width = tokens.shape[1]
    hidden = w_gate.shape[2]
    half = width // 2
    dma = pltpu.SemaphoreType.DMA
    vmem = pl.BlockSpec(memory_space=pltpu.VMEM)
    hbm = pl.BlockSpec(memory_space=pl.ANY)
    return pl.pallas_call(
        layer_kernel,
        out_shape=(
            jax.ShapeDtypeStruct((128, half), BF),
            jax.ShapeDtypeStruct((1, width, hidden), BF),
            jax.ShapeDtypeStruct((1, width, hidden), BF),
            jax.ShapeDtypeStruct((1, hidden, width), BF),
        ),
        in_specs=[hbm, hbm, vmem, vmem, hbm, hbm, hbm],
        out_specs=(vmem, hbm, hbm, hbm),
        scratch_shapes=[
            pltpu.VMEM((16, 128, width), BF),
            pltpu.VMEM((16, 16, 128), BF),
            pltpu.VMEM((SLOTS, 4, CAP, width), BF),
            pltpu.VMEM((2, 16, 4, CAP, width), BF),
            pltpu.VMEM((width, 2 * hidden), BF),
            pltpu.VMEM((hidden, width), BF),
            pltpu.VMEM((2048, hidden), BF),
            pltpu.VMEM((2048, 2 * hidden), BF),
            pltpu.VMEM((256, 2 * hidden), F32),
            pltpu.VMEM((256, hidden), F32),
            pltpu.VMEM((2, 2, 4, CAP, half), BF),
            pltpu.VMEM((8, 2, 4, CAP, half), BF),
            pltpu.VMEM((256, half), F32),
            pltpu.VMEM((EARLY, 4, CAP, half), BF),
            pltpu.VMEM((2, 4, CAP, half), BF),
            pltpu.VMEM((4, 16, 128), F32),
            pltpu.VMEM((4, EARLY * CAP, 128), BF),
            pltpu.VMEM((8 * CAP, 128), BF),
            pltpu.VMEM((3, 128, half), BF),
            pltpu.VMEM((3, 128, half), BF),
            pltpu.VMEM((2, 512, 2 * hidden), BF),
            pltpu.VMEM((2, hidden, 512), BF),
            dma((20,)), dma((16, 2)), dma((16,)), dma((16,)), dma((48,)), dma((48,)), dma((16,)), dma((16,)),
            dma((8,)), dma((8,)), dma((EARLY,)), dma((EARLY,)), dma((2, 4)), dma((2, 4)),
            dma((3,)), dma((3,)), dma((3,)), dma((3,)), dma((3,)), dma((2, 4)), dma((4,)), pltpu.SemaphoreType.DMA,
        ],
        compiler_params=pltpu.CompilerParams(collective_id=0, has_side_effects=True, vmem_limit_bytes=67043328),
    )(tokens, cotangent, meta, ranks, w_gate, w_up, w_down)


def routing(routes, gates):
    ids = jnp.arange(64, dtype=jnp.int32)
    hit = ids[:, None, None] == routes.T[None]
    mask = jnp.sum(hit.astype(F32), axis=1)
    gmap = jnp.sum(jnp.where(hit, gates.T[None], 0.0), axis=1)
    before = jnp.triu(jnp.ones((128, 128), BF), 1)
    rank = jnp.dot(mask.astype(BF), before, preferred_element_type=F32)
    rank = jnp.where(mask > 0, rank, 64.0)
    high = lax.reduce_precision(gmap, 8, 7)
    rest = gmap - high
    mid = lax.reduce_precision(rest, 8, 7)
    low = rest - mid
    return rank, jnp.stack([rank, high, mid, low]).astype(BF)


def body(tokens, cotangent, routes, gates, gate_weight, up_weight, down_weight):
    rank, maps = routing(routes, gates)
    meta = maps.reshape(4, 16, 4, 128).transpose(1, 0, 2, 3).reshape(16, 16, 128)
    ranks = rank.reshape(16, 4, 128).transpose(1, 0, 2)
    return layer(tokens, cotangent, meta, ranks, gate_weight, up_weight, down_weight)


def solution(mesh):
    in_specs = (
        P(("expert", "replica"), None),
        P(("expert", "replica"), None),
        P(("expert", "replica"), None),
        P(("expert", "replica"), None),
        P("expert", None, "tensor"),
        P("expert", None, "tensor"),
        P("expert", "tensor", None),
    )
    out_specs = (
        P(("expert", "replica"), "tensor"),
        P(("expert", "replica"), None, "tensor"),
        P(("expert", "replica"), None, "tensor"),
        P(("expert", "replica"), "tensor", None),
    )
    return jax.shard_map(body, mesh=mesh, in_specs=in_specs, out_specs=out_specs, check_vma=False)
```

```python
import jax
import jax.numpy as jnp
from jax import lax
from jax.experimental import pallas as pl
from jax.experimental.pallas import tpu as pltpu
from jax.sharding import PartitionSpec as P

MESH = pl.DeviceIdType.MESH
CAP = 32
BF = jnp.bfloat16
F32 = jnp.float32
LAG = 4
SLOTS = 8
ORDER = ((0, 0), (0, 1), (1, 0), (0, 2), (2, 0), (1, 1), (3, 3), (2, 1),
         (1, 2), (3, 2), (2, 3), (2, 2), (1, 3), (3, 1), (0, 3), (3, 0))
EARLY = 14


def entry(r, column):
    if isinstance(r, int):
        return ORDER[r][column]
    found = 0
    for k, pair in enumerate(ORDER):
        if pair[column]:
            found = found + jnp.where(r == k, pair[column], 0)
    return found


def offset(r):
    return entry(r, 0), entry(r, 1)


def dot(a, b, ca, cb):
    return lax.dot_general(a, b, (((ca,), (cb,)), ((), ())), preferred_element_type=F32)


def layer_kernel(token_ref, cot_ref, meta_ref, rank_ref, wg_ref, wu_ref, wd_ref,
                 tok_ref, og_ref, ou_ref, od_ref,
                 ag, mag, stage, rows, wgu, wd, hid, grads, gu, hg, psend, precv, own, back,
                 last, xrank, place, lplace, xsend, xrecv, gacc, dacc, gtile, dtile,
                 ag_s, ag_r, mg_s, mg_r, x_s, x_r, f_s, f_r, p_s, p_r, b_s, b_r, l_s, l_r, k_s, k_r, t_s, t_r, w_s, og_s, od_s, i_s):
    e = lax.axis_index("expert")
    x = lax.axis_index("replica")
    c = lax.axis_index("tensor")
    y, z = e // 4, e % 4
    first = c == 0
    width = token_ref.shape[1]
    half = width // 2
    hidden = wd.shape[0]

    def chip(dy, dz):
        return ((y + dy + 4) % 4) * 4 + (z + dz + 4) % 4

    def remote(src, dst, send, recv, dev):
        return pltpu.make_async_remote_copy(src_ref=src, dst_ref=dst, send_sem=send, recv_sem=recv,
                                            device_id=dev, device_id_type=MESH)

    def at(a, b):
        return jnp.where(first, b, a), jnp.where(first, a, b)

    partner = (e, x, 1 - c)

    def weights():
        return (pltpu.make_async_copy(wg_ref.at[x], wgu.at[:, pl.ds(0, hidden)], w_s.at[0]),
                pltpu.make_async_copy(wu_ref.at[x], wgu.at[:, pl.ds(hidden, hidden)], w_s.at[1]),
                pltpu.make_async_copy(wd_ref.at[x], wd, w_s.at[2]))

    @pl.when(first)
    def _():
        pltpu.make_async_copy(token_ref, ag.at[e], i_s).start()

    @pl.when(jnp.logical_not(first))
    def _():
        pltpu.make_async_copy(cot_ref, ag.at[e], i_s).start()

    barrier = pltpu.get_barrier_semaphore()
    for rel in range(1, 16):
        pl.semaphore_signal(barrier, inc=1, device_id=(chip(rel // 4, rel % 4), x, c), device_id_type=MESH)
    for d in (1, 2, 3):
        pl.semaphore_signal(barrier, inc=1, device_id=(e, (x + d) % 4, c), device_id_type=MESH)
        for r in (14, 15):
            dy, dz = ORDER[r]
            pl.semaphore_signal(barrier, inc=1, device_id=(chip(dy, dz), (x + d) % 4, c), device_id_type=MESH)
            pl.semaphore_signal(barrier, inc=1, device_id=(chip(-dy, -dz), (x + d) % 4, c), device_id_type=MESH)
    pl.semaphore_signal(barrier, inc=1, device_id=partner, device_id_type=MESH)
    pltpu.make_async_copy(token_ref, ag.at[e], i_s).wait()
    pl.semaphore_wait(barrier, 31)

    def meta_copy(rel):
        dy, dz = rel // 4, rel % 4
        target = chip(dy, dz)
        landed = ((4 - dy) % 4) * 4 + (4 - dz) % 4
        return remote(meta_ref.at[target], mag.at[e], mg_s.at[rel], mg_r.at[landed], (target, x, c))

    def block_copy(a, b, da, db, slot, part=None):
        by, bz = at(a, b)
        ty, tz = at(da, db)
        home = chip(by, bz)
        landed = ((by - ty + 4) % 4) * 4 + (bz - tz + 4) % 4
        if part is None:
            piece, recv = ag.at[home], ag_r.at[landed, 0]
        else:
            piece, recv = ag.at[home, pl.ds(part * 64, 64)], ag_r.at[landed, part]
        return remote(piece, piece, ag_s.at[slot], recv, (chip(ty, tz), x, c))

    def wait_block(a, b, parts=False):
        by, bz = at(a, b)
        rel, home = by * 4 + bz, chip(by, bz)
        if parts:
            for part in range(2):
                piece = ag.at[home, pl.ds(part * 64, 64)]
                remote(piece, piece, ag_s.at[0], ag_r.at[rel, part], partner).wait_recv()
        else:
            remote(ag.at[home], ag.at[home], ag_s.at[0], ag_r.at[rel, 0], partner).wait_recv()

    def relay(a, slot):
        wait_block(a, 1)
        block_copy(a, 1, 0, 3, slot, 0).start()
        wait_block(a, 3)
        block_copy(a, 3, 0, 1, slot + 1, 1).start()

    def gather(s):
        @pl.when(s == 1)
        def _():
            wait_block(1, 0)
            block_copy(1, 0, 3, 0, 4, 0).start()
            wait_block(3, 0)
            block_copy(3, 0, 1, 0, 5, 1).start()
            block_copy(1, 0, 0, 1, 6).start()
            block_copy(1, 0, 0, 3, 7).start()
            block_copy(3, 0, 0, 1, 8).start()
            block_copy(3, 0, 0, 3, 9).start()
            relay(0, 12)
            for rel in range(1, 16):
                meta_copy(rel).wait_recv()

        @pl.when(s == 3)
        def _():
            wait_block(2, 0, True)
            block_copy(2, 0, 0, 1, 10).start()
            block_copy(2, 0, 0, 3, 11).start()

        @pl.when(s == 5)
        def _():
            relay(1, 14)
            relay(3, 16)

        @pl.when(s == 7)
        def _():
            relay(2, 18)

    for rel in range(1, 16):
        meta_copy(rel).start()
    for i, (da, db) in enumerate(((1, 0), (3, 0), (0, 1), (0, 3))):
        block_copy(0, 0, da, db, i).start()

    def rank_copy(d):
        return remote(rank_ref.at[(x + d) % 4], xrank.at[x], k_s.at[d - 1], k_r.at[d - 1], (e, (x + d) % 4, c))

    def rank_landed(d):
        return remote(rank_ref.at[0], xrank.at[(x - d + 4) % 4], k_s.at[d - 1], k_r.at[d - 1], partner)

    for d in (1, 2, 3):
        rank_copy(d).start()
    xrank[x] = rank_ref[x]
    mag[e] = meta_ref[e]
    for cp in weights():
        cp.start()

    def x_copy(r, d):
        return remote(stage.at[r % SLOTS, (x + d) % 4], rows.at[c, r, x], x_s.at[r * 3 + d - 1],
                      x_r.at[r * 3 + d - 1], (e, (x + d) % 4, c))

    def x_landed(r, d):
        return remote(stage.at[0, 0], rows.at[c, r, (x - d + 4) % 4], x_s.at[r * 3 + d - 1],
                      x_r.at[r * 3 + d - 1], partner)

    def forward(r, kind):
        return remote(rows.at[kind, r], rows.at[kind, r], f_s.at[r], f_r.at[r], partner)

    slot_ids = lax.broadcasted_iota(jnp.int32, (CAP, 128), 0).astype(F32)

    def pick(r, home):
        m = mag[home].astype(F32)
        gsum = m[4:8] + m[8:12] + m[12:16]
        sel, scale = [], []
        for j in range(4):
            s = jnp.where(slot_ids == m[j:j + 1], 1.0, 0.0)
            sel.append(s)
            scale.append(jnp.sum(s * gsum[j:j + 1], axis=1, keepdims=True))
        sel = jnp.concatenate(sel, axis=0).astype(BF)
        scale = jnp.concatenate(scale, axis=0)
        scale = jnp.where(first, jnp.ones_like(scale), scale)
        for t in range(0, width, 512):
            got = dot(sel, ag[home, :, t:t + 512], 1, 0) * scale
            stage[r % SLOTS, :, :, t:t + 512] = got.astype(BF).reshape(4, CAP, 512)

    def pair_copy(q):
        return remote(psend.at[q % 2], precv.at[q], p_s.at[q], p_r.at[q], partner)

    def back_copy(r):
        dy, dz = offset(r)
        return remote(precv.at[r // 2, r % 2], back.at[r], b_s.at[r], b_r.at[r], (chip(dy, dz), x, c))

    def last_copy(i, d):
        dy, dz = ORDER[EARLY + i]
        return remote(precv.at[7, i, (x + d) % 4], last.at[i, x], l_s.at[i, d], l_r.at[i, d],
                      (chip(dy, dz), (x + d) % 4, c))

    def last_landed(i, d):
        return remote(precv.at[7, i, 0], last.at[i, (x - d + 4) % 4], l_s.at[i, d], l_r.at[i, d], partner)

    def chunk(q):
        for i in range(2):
            forward(q * 2 + i, 1 - c).wait_recv()

        @pl.when(q == 0)
        def _():
            for cp in weights():
                cp.wait()

        gu[...] = dot(rows[0, pl.ds(q * 2, 2)].reshape(256, width), wgu[...], 1, 0)
        hg[...] = dot(rows[1, pl.ds(q * 2, 2)].reshape(256, width), wd[...], 1, 1)

        def act(i, carry):
            at = pl.multiple_of(i * 128, 128)
            to = pl.multiple_of(q * 256 + i * 128, 128)
            for t in range(0, hidden, 128):
                g = gu[pl.ds(at, 128), t:t + 128]
                u = gu[pl.ds(at, 128), hidden + t:hidden + t + 128]
                h = hg[pl.ds(at, 128), t:t + 128]
                s = jax.nn.sigmoid(g)
                a = g * s
                hid[pl.ds(to, 128), t:t + 128] = (a * u).astype(BF)
                grads[pl.ds(to, 128), t:t + 128] = (h * u * s * (1.0 + g * (1.0 - s))).astype(BF)
                grads[pl.ds(to, 128), hidden + t:hidden + t + 128] = (h * a).astype(BF)
            return carry

        lax.fori_loop(0, 2, act, 0)

        @pl.when(q >= 2)
        def _():
            pair_copy(q - 2).wait_send()

        mine = grads[pl.ds(pl.multiple_of(q * 256, 256), 256), :]
        for t in range(0, half, 512):
            w = wgu[pl.ds(pl.multiple_of((1 - c) * half + t, 512), 512), :]
            psend[q % 2, :, :, :, t:t + 512] = dot(mine, w, 1, 1).astype(BF).reshape(2, 4, CAP, 512)
        pair_copy(q).start()
        for t in range(0, half, 512):
            w = wgu[pl.ds(pl.multiple_of(c * half + t, 512), 512), :]
            own[:, t:t + 512] = dot(mine, w, 1, 1)
        pair_copy(q).wait_recv()
        for i in range(2):
            for t in range(0, half, 512):
                both = own[i * 128:(i + 1) * 128, t:t + 512].reshape(4, CAP, 512) + precv[q, i, :, :, t:t + 512].astype(F32)
                precv[q, i, :, :, t:t + 512] = both.astype(BF)
        for i in range(2):
            @pl.when((q < 7) & (q + i > 0))
            def _():
                back_copy(q * 2 + i).start()

        @pl.when(q == 0)
        def _():
            back[0] = precv[0, 0]

        @pl.when(q == 7)
        def _():
            for d in (2, 1, 3, 0):
                for i in range(2):
                    last_copy(i, d).start()

    def finish(r):
        for d in (1, 2, 3):
            x_landed(r, d).wait_recv()
        forward(r, c).start()

    def produce(r):
        dy, dz = offset(r)

        @pl.when(jnp.where(first, dy, dz) == 2)
        def _():
            wait_block(jnp.where(first, dz, dy), 2, True)

        @pl.when(r >= SLOTS)
        def _():
            for d in (1, 2, 3):
                x_copy(r - SLOTS, d).wait_send()

        pick(r, chip(dy, dz))
        for d in (1, 3, 2):
            x_copy(r, d).start()
        rows[c, r, x] = stage[r % SLOTS, x]

    def combine(k, t):
        return dot(place[k], back[:, pl.ds(k, 1), :, t:t + 512].reshape(EARLY * CAP, 512), 0, 0)

    def sum_copy(d):
        return remote(xsend.at[d - 1], xrecv.at[d - 1], t_s.at[d - 1], t_r.at[d - 1], (e, (x + d) % 4, c))

    def places():
        for d in (1, 2, 3):
            rank_landed(d).wait_recv()
        for r in range(EARLY):
            dy, dz = ORDER[r]
            for k in range(4):
                m = xrank[k, pl.ds(chip(-dy, -dz), 1), :]
                place[k, r * CAP:(r + 1) * CAP, :] = jnp.where(slot_ids == m, 1.0, 0.0).astype(BF)
        for i in range(2):
            dy, dz = ORDER[EARLY + i]
            for k in range(4):
                m = rank_ref[k, pl.ds(chip(-dy, -dz), 1), :]
                lplace[(i * 4 + k) * CAP:(i * 4 + k + 1) * CAP, :] = jnp.where(slot_ids == m, 1.0, 0.0).astype(BF)

    def early_sums():
        def waits(r, carry):
            back_copy(r).wait_recv()
            return carry

        lax.fori_loop(1, EARLY, waits, 0)
        for d in (2, 1, 3):
            for t in range(0, half, 512):
                xsend[d - 1, :, t:t + 512] = combine((x + d) % 4, t).astype(BF)
            sum_copy(d).start()

    def grad_part(k, cols):
        span = pl.ds(pl.multiple_of(k * 512, 512), 512)
        blocks = pl.ds(k * 4, 4)
        return (dot(rows[0, blocks, :, :, cols].reshape(512, 512), grads[span, :], 0, 0),
                dot(hid[span, :], rows[1, blocks, :, :, cols].reshape(512, 512), 0, 0))

    def accumulate(k):
        for t in range(4):
            cols = slice(t * 512, (t + 1) * 512)
            more_g, more_d = grad_part(k, cols)
            gacc[cols, :] = gacc[cols, :] + more_g
            dacc[:, cols] = dacc[:, cols] + more_d

    gacc[...] = jnp.zeros_like(gacc)
    dacc[...] = jnp.zeros_like(dacc)

    def step(s, carry):
        @pl.when(s < 16)
        def _():
            gather(s)
            produce(s)

        @pl.when((s >= LAG) & (s < 16 + LAG))
        def _():
            finish(s - LAG)

        @pl.when(s == 9)
        def _():
            places()

        @pl.when((s > LAG) & ((s - LAG) % 2 == 0))
        def _():
            chunk((s - LAG) // 2 - 1)

        @pl.when((s > LAG) & (s < 16 + LAG) & ((s - LAG) % 4 == 0))
        def _():
            accumulate((s - LAG) // 4 - 1)
        return carry

    lax.fori_loop(0, 17 + LAG, step, 0)
    early_sums()

    def grad_out(t):
        at = pl.ds(pl.multiple_of(t * 512, 512), 512)
        return (pltpu.make_async_copy(gtile.at[t % 2, :, pl.ds(0, hidden)], og_ref.at[0, at, :], og_s.at[0, t]),
                pltpu.make_async_copy(gtile.at[t % 2, :, pl.ds(hidden, hidden)], ou_ref.at[0, at, :], og_s.at[1, t]),
                pltpu.make_async_copy(dtile.at[t % 2], od_ref.at[0, :, at], od_s.at[t]))

    for t in range(4):
        cols = slice(t * 512, (t + 1) * 512)
        if t >= 2:
            for cp in grad_out(t - 2):
                cp.wait()
        more_g, more_d = grad_part(3, cols)
        gtile[t % 2] = (gacc[cols, :] + more_g).astype(BF)
        dtile[t % 2] = (dacc[:, cols] + more_d).astype(BF)
        for cp in grad_out(t):
            cp.start()

    for t in range(0, half, 512):
        own[0:128, t:t + 512] = combine(x, t)
    for d in (1, 3, 2):
        sum_copy(d).wait_recv()
        own[0:128, :] = own[0:128, :] + xrecv[d - 1].astype(F32)
    for i in range(2):
        for d in range(4):
            last_landed(i, d).wait_recv()
    for t in range(0, half, 512):
        got = dot(lplace[...], last[:, :, :, t:t + 512].reshape(8 * CAP, 512), 0, 0)
        tok_ref[:, t:t + 512] = (own[0:128, t:t + 512] + got).astype(BF)

    def close(r, carry):
        forward(r, c).wait_send()

        @pl.when(r >= 16 - SLOTS)
        def _():
            for d in (1, 2, 3):
                x_copy(r, d).wait_send()

        @pl.when((r >= 1) & (r < EARLY))
        def _():
            back_copy(r).wait_send()
        return carry

    lax.fori_loop(0, 16, close, 0)
    for i in range(2):
        for d in range(4):
            last_copy(i, d).wait_send()
    for slot in range(20):
        half_sent = slot in (4, 5) or slot >= 12
        block_copy(0, 0, 1, 0, slot, 0 if half_sent else None).wait_send()
    for rel in range(1, 16):
        meta_copy(rel).wait_send()
    for d in (1, 2, 3):
        rank_copy(d).wait_send()
        sum_copy(d).wait_send()
    for q in (6, 7):
        pair_copy(q).wait_send()
    for t in (2, 3):
        for cp in grad_out(t):
            cp.wait()


def layer(tokens, cotangent, meta, ranks, w_gate, w_up, w_down):
    width = tokens.shape[1]
    hidden = w_gate.shape[2]
    half = width // 2
    dma = pltpu.SemaphoreType.DMA
    vmem = pl.BlockSpec(memory_space=pltpu.VMEM)
    hbm = pl.BlockSpec(memory_space=pl.ANY)
    return pl.pallas_call(
        layer_kernel,
        out_shape=(
            jax.ShapeDtypeStruct((128, half), BF),
            jax.ShapeDtypeStruct((1, width, hidden), BF),
            jax.ShapeDtypeStruct((1, width, hidden), BF),
            jax.ShapeDtypeStruct((1, hidden, width), BF),
        ),
        in_specs=[hbm, hbm, vmem, vmem, hbm, hbm, hbm],
        out_specs=(vmem, hbm, hbm, hbm),
        scratch_shapes=[
            pltpu.VMEM((16, 128, width), BF),
            pltpu.VMEM((16, 16, 128), BF),
            pltpu.VMEM((SLOTS, 4, CAP, width), BF),
            pltpu.VMEM((2, 16, 4, CAP, width), BF),
            pltpu.VMEM((width, 2 * hidden), BF),
            pltpu.VMEM((hidden, width), BF),
            pltpu.VMEM((2048, hidden), BF),
            pltpu.VMEM((2048, 2 * hidden), BF),
            pltpu.VMEM((256, 2 * hidden), F32),
            pltpu.VMEM((256, hidden), F32),
            pltpu.VMEM((2, 2, 4, CAP, half), BF),
            pltpu.VMEM((8, 2, 4, CAP, half), BF),
            pltpu.VMEM((256, half), F32),
            pltpu.VMEM((EARLY, 4, CAP, half), BF),
            pltpu.VMEM((2, 4, CAP, half), BF),
            pltpu.VMEM((4, 16, 128), F32),
            pltpu.VMEM((4, EARLY * CAP, 128), BF),
            pltpu.VMEM((8 * CAP, 128), BF),
            pltpu.VMEM((3, 128, half), BF),
            pltpu.VMEM((3, 128, half), BF),
            pltpu.VMEM((width, 2 * hidden), F32),
            pltpu.VMEM((hidden, width), F32),
            pltpu.VMEM((2, 512, 2 * hidden), BF),
            pltpu.VMEM((2, hidden, 512), BF),
            dma((20,)), dma((16, 2)), dma((16,)), dma((16,)), dma((48,)), dma((48,)), dma((16,)), dma((16,)),
            dma((8,)), dma((8,)), dma((EARLY,)), dma((EARLY,)), dma((2, 4)), dma((2, 4)),
            dma((3,)), dma((3,)), dma((3,)), dma((3,)), dma((3,)), dma((2, 4)), dma((4,)), pltpu.SemaphoreType.DMA,
        ],
        compiler_params=pltpu.CompilerParams(collective_id=0, has_side_effects=True, vmem_limit_bytes=67043328),
    )(tokens, cotangent, meta, ranks, w_gate, w_up, w_down)


def routing(routes, gates):
    ids = jnp.arange(64, dtype=jnp.int32)
    hit = ids[:, None, None] == routes.T[None]
    mask = jnp.sum(hit.astype(F32), axis=1)
    gmap = jnp.sum(jnp.where(hit, gates.T[None], 0.0), axis=1)
    before = jnp.triu(jnp.ones((128, 128), BF), 1)
    rank = jnp.dot(mask.astype(BF), before, preferred_element_type=F32)
    rank = jnp.where(mask > 0, rank, 64.0)
    high = lax.reduce_precision(gmap, 8, 7)
    rest = gmap - high
    mid = lax.reduce_precision(rest, 8, 7)
    low = rest - mid
    return rank, jnp.stack([rank, high, mid, low]).astype(BF)


def body(tokens, cotangent, routes, gates, gate_weight, up_weight, down_weight):
    rank, maps = routing(routes, gates)
    meta = maps.reshape(4, 16, 4, 128).transpose(1, 0, 2, 3).reshape(16, 16, 128)
    ranks = rank.reshape(16, 4, 128).transpose(1, 0, 2)
    return layer(tokens, cotangent, meta, ranks, gate_weight, up_weight, down_weight)


def solution(mesh):
    in_specs = (
        P(("expert", "replica"), None),
        P(("expert", "replica"), None),
        P(("expert", "replica"), None),
        P(("expert", "replica"), None),
        P("expert", None, "tensor"),
        P("expert", None, "tensor"),
        P("expert", "tensor", None),
    )
    out_specs = (
        P(("expert", "replica"), "tensor"),
        P(("expert", "replica"), None, "tensor"),
        P(("expert", "replica"), None, "tensor"),
        P(("expert", "replica"), "tensor", None),
    )
    return jax.shard_map(body, mesh=mesh, in_specs=in_specs, out_specs=out_specs, check_vma=False)
```

```python
import jax
import jax.numpy as jnp
from jax import lax
from jax.experimental import pallas as pl
from jax.experimental.pallas import tpu as pltpu
from jax.sharding import PartitionSpec as P

MESH = pl.DeviceIdType.MESH
CAP = 32
BF = jnp.bfloat16
F32 = jnp.float32
LAG = 4
SLOTS = 8
ORDER = ((0, 0), (0, 1), (1, 0), (0, 2), (2, 0), (1, 1), (3, 3), (2, 1),
         (1, 2), (3, 2), (2, 3), (2, 2), (1, 3), (3, 1), (0, 3), (3, 0))
EARLY = 14
MIRRORED = (1, 3, 7, 9, 12, 14)


def entry(r, column):
    if isinstance(r, int):
        return ORDER[r][column]
    found = 0
    for k, pair in enumerate(ORDER):
        if pair[column]:
            found = found + jnp.where(r == k, pair[column], 0)
    return found


def offset(r):
    return entry(r, 0), entry(r, 1)


def dot(a, b, ca, cb):
    return lax.dot_general(a, b, (((ca,), (cb,)), ((), ())), preferred_element_type=F32)


def layer_kernel(token_ref, cot_ref, meta_ref, rank_ref, wg_ref, wu_ref, wd_ref,
                 tok_ref, og_ref, ou_ref, od_ref,
                 ag, mag, stage, rows, wgu, wd, hid, grads, gu, hg, psend, precv, own, back,
                 last, xrank, place, lplace, xsend, xrecv, gacc, dacc, gtile, dtile,
                 ag_s, ag_r, mg_s, mg_r, x_s, x_r, f_s, f_r, p_s, p_r, b_s, b_r, l_s, l_r, k_s, k_r, t_s, t_r, w_s, og_s, od_s, i_s):
    e = lax.axis_index("expert")
    x = lax.axis_index("replica")
    c = lax.axis_index("tensor")
    y, z = e // 4, e % 4
    first = c == 0
    width = token_ref.shape[1]
    half = width // 2
    hidden = wd.shape[0]

    def chip(dy, dz):
        return ((y + dy + 4) % 4) * 4 + (z + dz + 4) % 4

    def remote(src, dst, send, recv, dev):
        return pltpu.make_async_remote_copy(src_ref=src, dst_ref=dst, send_sem=send, recv_sem=recv,
                                            device_id=dev, device_id_type=MESH)

    def at(a, b):
        return jnp.where(first, b, a), jnp.where(first, a, b)

    partner = (e, x, 1 - c)

    def weights():
        return (pltpu.make_async_copy(wg_ref.at[x], wgu.at[:, pl.ds(0, hidden)], w_s.at[0]),
                pltpu.make_async_copy(wu_ref.at[x], wgu.at[:, pl.ds(hidden, hidden)], w_s.at[1]),
                pltpu.make_async_copy(wd_ref.at[x], wd, w_s.at[2]))

    @pl.when(first)
    def _():
        pltpu.make_async_copy(token_ref, ag.at[e], i_s).start()

    @pl.when(jnp.logical_not(first))
    def _():
        pltpu.make_async_copy(cot_ref, ag.at[e], i_s).start()

    barrier = pltpu.get_barrier_semaphore()
    for rel in range(1, 16):
        pl.semaphore_signal(barrier, inc=1, device_id=(chip(rel // 4, rel % 4), x, c), device_id_type=MESH)
    for d in (1, 2, 3):
        pl.semaphore_signal(barrier, inc=1, device_id=(e, (x + d) % 4, c), device_id_type=MESH)
        for r in (14, 15):
            dy, dz = ORDER[r]
            pl.semaphore_signal(barrier, inc=1, device_id=(chip(dy, dz), (x + d) % 4, c), device_id_type=MESH)
            pl.semaphore_signal(barrier, inc=1, device_id=(chip(-dy, -dz), (x + d) % 4, c), device_id_type=MESH)
    pl.semaphore_signal(barrier, inc=1, device_id=partner, device_id_type=MESH)
    pltpu.make_async_copy(token_ref, ag.at[e], i_s).wait()
    pl.semaphore_wait(barrier, 31)

    def meta_copy(rel):
        dy, dz = rel // 4, rel % 4
        target = chip(dy, dz)
        landed = ((4 - dy) % 4) * 4 + (4 - dz) % 4
        return remote(meta_ref.at[target], mag.at[e], mg_s.at[rel], mg_r.at[landed], (target, x, c))

    def block_copy(a, b, da, db, slot, part=None):
        by, bz = at(a, b)
        ty, tz = at(da, db)
        home = chip(by, bz)
        landed = ((by - ty + 4) % 4) * 4 + (bz - tz + 4) % 4
        if part is None:
            piece, recv = ag.at[home], ag_r.at[landed, 0]
        else:
            piece, recv = ag.at[home, pl.ds(part * 64, 64)], ag_r.at[landed, part]
        return remote(piece, piece, ag_s.at[slot], recv, (chip(ty, tz), x, c))

    def wait_block(a, b, parts=False):
        by, bz = at(a, b)
        rel, home = by * 4 + bz, chip(by, bz)
        if parts:
            for part in range(2):
                piece = ag.at[home, pl.ds(part * 64, 64)]
                remote(piece, piece, ag_s.at[0], ag_r.at[rel, part], partner).wait_recv()
        else:
            remote(ag.at[home], ag.at[home], ag_s.at[0], ag_r.at[rel, 0], partner).wait_recv()

    def relay(a, slot):
        wait_block(a, 1)
        block_copy(a, 1, 0, 3, slot, 0).start()
        wait_block(a, 3)
        block_copy(a, 3, 0, 1, slot + 1, 1).start()

    def gather(s):
        @pl.when(s == 1)
        def _():
            wait_block(1, 0)
            block_copy(1, 0, 3, 0, 4, 0).start()
            wait_block(3, 0)
            block_copy(3, 0, 1, 0, 5, 1).start()
            block_copy(0, 0, 0, 1, 2).start()
            block_copy(0, 0, 0, 3, 3).start()
            block_copy(1, 0, 0, 1, 6).start()
            block_copy(1, 0, 0, 3, 7).start()
            block_copy(3, 0, 0, 1, 8).start()
            block_copy(3, 0, 0, 3, 9).start()
            for rel in range(1, 16):
                meta_copy(rel).wait_recv()

        @pl.when(s == 2)
        def _():
            relay(0, 12)

        @pl.when(s == 3)
        def _():
            wait_block(2, 0, True)
            block_copy(2, 0, 0, 1, 10).start()
            block_copy(2, 0, 0, 3, 11).start()

        @pl.when(s == 5)
        def _():
            relay(1, 14)
            relay(3, 16)

        @pl.when(s == 7)
        def _():
            relay(2, 18)

    for rel in range(1, 16):
        meta_copy(rel).start()
    block_copy(0, 0, 1, 0, 0).start()
    block_copy(0, 0, 3, 0, 1).start()

    def rank_copy(d):
        return remote(rank_ref.at[(x + d) % 4], xrank.at[x], k_s.at[d - 1], k_r.at[d - 1], (e, (x + d) % 4, c))

    def rank_landed(d):
        return remote(rank_ref.at[0], xrank.at[(x - d + 4) % 4], k_s.at[d - 1], k_r.at[d - 1], partner)

    for d in (1, 2, 3):
        rank_copy(d).start()
    xrank[x] = rank_ref[x]
    mag[e] = meta_ref[e]
    for cp in weights():
        cp.start()

    def x_copy(r, d):
        return remote(stage.at[r % SLOTS, (x + d) % 4], rows.at[c, r, x], x_s.at[r * 3 + d - 1],
                      x_r.at[r * 3 + d - 1], (e, (x + d) % 4, c))

    def x_landed(r, d):
        return remote(stage.at[0, 0], rows.at[c, r, (x - d + 4) % 4], x_s.at[r * 3 + d - 1],
                      x_r.at[r * 3 + d - 1], partner)

    def forward(r, kind):
        return remote(rows.at[kind, r], rows.at[kind, r], f_s.at[r], f_r.at[r], partner)

    slot_ids = lax.broadcasted_iota(jnp.int32, (CAP, 128), 0).astype(F32)

    def pick(r, home):
        m = mag[home].astype(F32)
        gsum = m[4:8] + m[8:12] + m[12:16]
        sel, scale = [], []
        for j in range(4):
            s = jnp.where(slot_ids == m[j:j + 1], 1.0, 0.0)
            sel.append(s)
            scale.append(jnp.sum(s * gsum[j:j + 1], axis=1, keepdims=True))
        sel = jnp.concatenate(sel, axis=0).astype(BF)
        scale = jnp.concatenate(scale, axis=0)
        scale = jnp.where(first, jnp.ones_like(scale), scale)
        for t in range(0, width, 512):
            got = dot(sel, ag[home, :, t:t + 512], 1, 0) * scale
            stage[r % SLOTS, :, :, t:t + 512] = got.astype(BF).reshape(4, CAP, 512)

    def pair_copy(q):
        return remote(psend.at[q % 2], precv.at[q], p_s.at[q], p_r.at[q], partner)

    def back_copy(r):
        dy, dz = offset(r)
        return remote(precv.at[r // 2, r % 2], back.at[r], b_s.at[r], b_r.at[r], (chip(dy, dz), x, c))

    def last_copy(i, d):
        dy, dz = ORDER[EARLY + i]
        return remote(precv.at[7, i, (x + d) % 4], last.at[i, x], l_s.at[i, d], l_r.at[i, d],
                      (chip(dy, dz), (x + d) % 4, c))

    def last_landed(i, d):
        return remote(precv.at[7, i, 0], last.at[i, (x - d + 4) % 4], l_s.at[i, d], l_r.at[i, d], partner)

    def chunk(q):
        for i in range(2):
            forward(q * 2 + i, 1 - c).wait_recv()

        @pl.when(q == 0)
        def _():
            for cp in weights():
                cp.wait()

        gu[...] = dot(rows[0, pl.ds(q * 2, 2)].reshape(256, width), wgu[...], 1, 0)
        hg[...] = dot(rows[1, pl.ds(q * 2, 2)].reshape(256, width), wd[...], 1, 1)

        def act(i, carry):
            at = pl.multiple_of(i * 128, 128)
            to = pl.multiple_of(q * 256 + i * 128, 128)
            for t in range(0, hidden, 128):
                g = gu[pl.ds(at, 128), t:t + 128]
                u = gu[pl.ds(at, 128), hidden + t:hidden + t + 128]
                h = hg[pl.ds(at, 128), t:t + 128]
                s = jax.nn.sigmoid(g)
                a = g * s
                hid[pl.ds(to, 128), t:t + 128] = (a * u).astype(BF)
                grads[pl.ds(to, 128), t:t + 128] = (h * u * s * (1.0 + g * (1.0 - s))).astype(BF)
                grads[pl.ds(to, 128), hidden + t:hidden + t + 128] = (h * a).astype(BF)
            return carry

        lax.fori_loop(0, 2, act, 0)

        @pl.when(q >= 2)
        def _():
            pair_copy(q - 2).wait_send()

        mine = grads[pl.ds(pl.multiple_of(q * 256, 256), 256), :]
        for t in range(0, half, 512):
            w = wgu[pl.ds(pl.multiple_of((1 - c) * half + t, 512), 512), :]
            psend[q % 2, :, :, :, t:t + 512] = dot(mine, w, 1, 1).astype(BF).reshape(2, 4, CAP, 512)
        pair_copy(q).start()
        for t in range(0, half, 512):
            w = wgu[pl.ds(pl.multiple_of(c * half + t, 512), 512), :]
            own[:, t:t + 512] = dot(mine, w, 1, 1)
        pair_copy(q).wait_recv()
        for i in range(2):
            for t in range(0, half, 512):
                both = own[i * 128:(i + 1) * 128, t:t + 512].reshape(4, CAP, 512) + precv[q, i, :, :, t:t + 512].astype(F32)
                precv[q, i, :, :, t:t + 512] = both.astype(BF)
        for i in range(2):
            @pl.when((q < 7) & (q + i > 0))
            def _():
                back_copy(q * 2 + i).start()

        @pl.when(q == 0)
        def _():
            back[0] = precv[0, 0]

        @pl.when(q == 7)
        def _():
            for d in (2, 1, 3, 0):
                for i in range(2):
                    last_copy(i, d).start()

    def finish(r):
        for d in (1, 2, 3):
            x_landed(r, d).wait_recv()
        forward(r, c).start()

    def produce(r):
        dy, dz = offset(r)

        @pl.when(jnp.where(first, dy, dz) == 2)
        def _():
            wait_block(jnp.where(first, dz, dy), 2, True)

        @pl.when(r >= SLOTS)
        def _():
            for d in (1, 2, 3):
                x_copy(r - SLOTS, d).wait_send()

        pick(r, chip(dy, dz))
        for d in (1, 3, 2):
            x_copy(r, d).start()
        rows[c, r, x] = stage[r % SLOTS, x]

    def combine(k, t):
        return dot(place[k], back[:, pl.ds(k, 1), :, t:t + 512].reshape(EARLY * CAP, 512), 0, 0)

    def sum_copy(d):
        return remote(xsend.at[d - 1], xrecv.at[d - 1], t_s.at[d - 1], t_r.at[d - 1], (e, (x + d) % 4, c))

    def places():
        for d in (1, 2, 3):
            rank_landed(d).wait_recv()
        for r in range(EARLY):
            dy, dz = ORDER[r]
            for k in range(4):
                m = xrank[k, pl.ds(chip(-dy, -dz), 1), :]
                place[k, r * CAP:(r + 1) * CAP, :] = jnp.where(slot_ids == m, 1.0, 0.0).astype(BF)
        for i in range(2):
            dy, dz = ORDER[EARLY + i]
            for k in range(4):
                m = rank_ref[k, pl.ds(chip(-dy, -dz), 1), :]
                lplace[(i * 4 + k) * CAP:(i * 4 + k + 1) * CAP, :] = jnp.where(slot_ids == m, 1.0, 0.0).astype(BF)

    def early_sums():
        def waits(r, carry):
            back_copy(r).wait_recv()
            return carry

        lax.fori_loop(1, EARLY, waits, 0)
        for d in (2, 1, 3):
            for t in range(0, half, 512):
                xsend[d - 1, :, t:t + 512] = combine((x + d) % 4, t).astype(BF)
            sum_copy(d).start()

    def grad_part(k, cols):
        span = pl.ds(pl.multiple_of(k * 512, 512), 512)
        blocks = pl.ds(k * 4, 4)
        return (dot(rows[0, blocks, :, :, cols].reshape(512, 512), grads[span, :], 0, 0),
                dot(hid[span, :], rows[1, blocks, :, :, cols].reshape(512, 512), 0, 0))

    def accumulate(k):
        for t in range(4):
            cols = slice(t * 512, (t + 1) * 512)
            more_g, more_d = grad_part(k, cols)
            gacc[cols, :] = gacc[cols, :] + more_g
            dacc[:, cols] = dacc[:, cols] + more_d

    gacc[...] = jnp.zeros_like(gacc)
    dacc[...] = jnp.zeros_like(dacc)

    def turn(s):
        swap = 0
        for k in MIRRORED:
            swap = swap + jnp.where(s == k, 1, 0) - jnp.where(s == k + 1, 1, 0)
        return jnp.where(first, s, s + swap)

    def step(s, carry):
        @pl.when(s < 16)
        def _():
            gather(s)
            produce(turn(s))

        @pl.when((s >= LAG) & (s < 16 + LAG))
        def _():
            finish(turn(s - LAG))

        @pl.when(s == 9)
        def _():
            places()

        @pl.when((s > LAG) & ((s - LAG) % 2 == 0))
        def _():
            chunk((s - LAG) // 2 - 1)

        @pl.when((s > LAG) & (s < 16 + LAG) & ((s - LAG) % 4 == 0))
        def _():
            accumulate((s - LAG) // 4 - 1)
        return carry

    lax.fori_loop(0, 17 + LAG, step, 0)
    early_sums()

    def grad_out(t):
        at = pl.ds(pl.multiple_of(t * 512, 512), 512)
        return (pltpu.make_async_copy(gtile.at[t % 2, :, pl.ds(0, hidden)], og_ref.at[0, at, :], og_s.at[0, t]),
                pltpu.make_async_copy(gtile.at[t % 2, :, pl.ds(hidden, hidden)], ou_ref.at[0, at, :], og_s.at[1, t]),
                pltpu.make_async_copy(dtile.at[t % 2], od_ref.at[0, :, at], od_s.at[t]))

    for t in range(4):
        cols = slice(t * 512, (t + 1) * 512)
        if t >= 2:
            for cp in grad_out(t - 2):
                cp.wait()
        more_g, more_d = grad_part(3, cols)
        gtile[t % 2] = (gacc[cols, :] + more_g).astype(BF)
        dtile[t % 2] = (dacc[:, cols] + more_d).astype(BF)
        for cp in grad_out(t):
            cp.start()

    for t in range(0, half, 512):
        own[0:128, t:t + 512] = combine(x, t)
    for d in (1, 3, 2):
        sum_copy(d).wait_recv()
        own[0:128, :] = own[0:128, :] + xrecv[d - 1].astype(F32)
    for i in range(2):
        for d in range(4):
            last_landed(i, d).wait_recv()
    for t in range(0, half, 512):
        got = dot(lplace[...], last[:, :, :, t:t + 512].reshape(8 * CAP, 512), 0, 0)
        tok_ref[:, t:t + 512] = (own[0:128, t:t + 512] + got).astype(BF)

    def close(r, carry):
        forward(r, c).wait_send()

        @pl.when(r >= 16 - SLOTS)
        def _():
            for d in (1, 2, 3):
                x_copy(r, d).wait_send()

        @pl.when((r >= 1) & (r < EARLY))
        def _():
            back_copy(r).wait_send()
        return carry

    lax.fori_loop(0, 16, close, 0)
    for i in range(2):
        for d in range(4):
            last_copy(i, d).wait_send()
    for slot in range(20):
        half_sent = slot in (4, 5) or slot >= 12
        block_copy(0, 0, 1, 0, slot, 0 if half_sent else None).wait_send()
    for rel in range(1, 16):
        meta_copy(rel).wait_send()
    for d in (1, 2, 3):
        rank_copy(d).wait_send()
        sum_copy(d).wait_send()
    for q in (6, 7):
        pair_copy(q).wait_send()
    for t in (2, 3):
        for cp in grad_out(t):
            cp.wait()


def layer(tokens, cotangent, meta, ranks, w_gate, w_up, w_down):
    width = tokens.shape[1]
    hidden = w_gate.shape[2]
    half = width // 2
    dma = pltpu.SemaphoreType.DMA
    vmem = pl.BlockSpec(memory_space=pltpu.VMEM)
    hbm = pl.BlockSpec(memory_space=pl.ANY)
    return pl.pallas_call(
        layer_kernel,
        out_shape=(
            jax.ShapeDtypeStruct((128, half), BF),
            jax.ShapeDtypeStruct((1, width, hidden), BF),
            jax.ShapeDtypeStruct((1, width, hidden), BF),
            jax.ShapeDtypeStruct((1, hidden, width), BF),
        ),
        in_specs=[hbm, hbm, vmem, vmem, hbm, hbm, hbm],
        out_specs=(vmem, hbm, hbm, hbm),
        scratch_shapes=[
            pltpu.VMEM((16, 128, width), BF),
            pltpu.VMEM((16, 16, 128), BF),
            pltpu.VMEM((SLOTS, 4, CAP, width), BF),
            pltpu.VMEM((2, 16, 4, CAP, width), BF),
            pltpu.VMEM((width, 2 * hidden), BF),
            pltpu.VMEM((hidden, width), BF),
            pltpu.VMEM((2048, hidden), BF),
            pltpu.VMEM((2048, 2 * hidden), BF),
            pltpu.VMEM((256, 2 * hidden), F32),
            pltpu.VMEM((256, hidden), F32),
            pltpu.VMEM((2, 2, 4, CAP, half), BF),
            pltpu.VMEM((8, 2, 4, CAP, half), BF),
            pltpu.VMEM((256, half), F32),
            pltpu.VMEM((EARLY, 4, CAP, half), BF),
            pltpu.VMEM((2, 4, CAP, half), BF),
            pltpu.VMEM((4, 16, 128), F32),
            pltpu.VMEM((4, EARLY * CAP, 128), BF),
            pltpu.VMEM((8 * CAP, 128), BF),
            pltpu.VMEM((3, 128, half), BF),
            pltpu.VMEM((3, 128, half), BF),
            pltpu.VMEM((width, 2 * hidden), F32),
            pltpu.VMEM((hidden, width), F32),
            pltpu.VMEM((2, 512, 2 * hidden), BF),
            pltpu.VMEM((2, hidden, 512), BF),
            dma((20,)), dma((16, 2)), dma((16,)), dma((16,)), dma((48,)), dma((48,)), dma((16,)), dma((16,)),
            dma((8,)), dma((8,)), dma((EARLY,)), dma((EARLY,)), dma((2, 4)), dma((2, 4)),
            dma((3,)), dma((3,)), dma((3,)), dma((3,)), dma((3,)), dma((2, 4)), dma((4,)), pltpu.SemaphoreType.DMA,
        ],
        compiler_params=pltpu.CompilerParams(collective_id=0, has_side_effects=True, vmem_limit_bytes=67043328),
    )(tokens, cotangent, meta, ranks, w_gate, w_up, w_down)


def routing(routes, gates):
    ids = jnp.arange(64, dtype=jnp.int32)
    hit = ids[:, None, None] == routes.T[None]
    mask = jnp.sum(hit.astype(F32), axis=1)
    gmap = jnp.sum(jnp.where(hit, gates.T[None], 0.0), axis=1)
    before = jnp.triu(jnp.ones((128, 128), BF), 1)
    rank = jnp.dot(mask.astype(BF), before, preferred_element_type=F32)
    rank = jnp.where(mask > 0, rank, 64.0)
    high = lax.reduce_precision(gmap, 8, 7)
    rest = gmap - high
    mid = lax.reduce_precision(rest, 8, 7)
    low = rest - mid
    return rank, jnp.stack([rank, high, mid, low]).astype(BF)


def body(tokens, cotangent, routes, gates, gate_weight, up_weight, down_weight):
    rank, maps = routing(routes, gates)
    meta = maps.reshape(4, 16, 4, 128).transpose(1, 0, 2, 3).reshape(16, 16, 128)
    ranks = rank.reshape(16, 4, 128).transpose(1, 0, 2)
    return layer(tokens, cotangent, meta, ranks, gate_weight, up_weight, down_weight)


def solution(mesh):
    in_specs = (
        P(("expert", "replica"), None),
        P(("expert", "replica"), None),
        P(("expert", "replica"), None),
        P(("expert", "replica"), None),
        P("expert", None, "tensor"),
        P("expert", None, "tensor"),
        P("expert", "tensor", None),
    )
    out_specs = (
        P(("expert", "replica"), "tensor"),
        P(("expert", "replica"), None, "tensor"),
        P(("expert", "replica"), None, "tensor"),
        P(("expert", "replica"), "tensor", None),
    )
    return jax.shard_map(body, mesh=mesh, in_specs=in_specs, out_specs=out_specs, check_vma=False)
```
